128 devices in a mesh: sky: 16 (over x, z), depth: 8 (over y, core).
Axes of the slice: x: 4, y: 4, z: 4, core: 2. Of those that a mesh axis runs over, the one named last changes fastest.
Arguments:
- positions: float32 [3, 2048, 128], P(None, ('sky', 'depth')), may hold values from 0 to 1
- cell_points: int32 [2048], P(('sky', 'depth')), may hold values from 1 to 128
- target_log: float32 [16], replicated, may hold values from 8 to 20
- export_count: int32 [128, 128], P(('sky', 'depth')), may hold values from 0 to 3, as said below
- export_cell: int32 [128, 128, 3], P(('sky', 'depth')), may hold values from 0 to 15
- import_pair: int32 [128, 128, 3], P(('sky', 'depth')), may hold values from 0 to 15
- import_shift: int32 [3, 128, 128, 3], P(None, ('sky', 'depth')), may hold values from -1 to 1, as said below
Outputs:
- travel: float32 [3, 2048, 128], P(None, ('sky', 'depth'))
The draws below stay inside these ranges and needn't reach their ends.
Inputs may be any that keep to these rules, and one draw needn't show every extreme that they name: export_count[s, t] counts the slots of export_cell[s, t] that are used; it is zero unless s and t are distinct devices whose sky indices differ by at most one modulo the sky axis's size and whose depth indices differ by at most one; in every draw some device t receives 3 cells from each such neighbour. For neighbouring devices t and s, components 0 and 2 of import_shift[:, t, s, k] are the sky step and the depth step from t's region to s's region (sky taken around the cycle), component 1 varies; all components are zero for devices that are not neighbours.
All inputs are finite; a program needn't handle non-finite values.
Results may differ from the reference program's by a relative error of at most 0.00022.
Values sent between devices are 32-bit elements; how exact they have to be, the bound alone decides.
No kernel may reach another device: no remote copies, remote signals or barrier semaphores. Data moves between devices by JAX's collectives and lax.ppermute only.
A program may use at most 64 MiB of HBM per device.

```python
import jax
import jax.numpy as jnp
from jax import lax

PTS = 128
BINS = 16
SLOTS = 3
STEPS = 2
CELL_DEV = 16
PEERS = 128
CELLS = 2048
N_SKY = 16
N_DEPTH = 8


def region_steps():
    device_ids = jnp.arange(PEERS, dtype=jnp.int32)
    sky_ids = device_ids // N_DEPTH
    depth_ids = device_ids % N_DEPTH
    sky_step = (sky_ids[None, :] - sky_ids[:, None] + 1) % N_SKY - 1
    depth_step = depth_ids[None, :] - depth_ids[:, None]
    near = (jnp.abs(sky_step) <= 1) & (jnp.abs(depth_step) <= 1) & (device_ids[None, :] != device_ids[:, None])
    return (sky_step, depth_step, near)


def draw_export_count(key, part):
    sky_step, depth_step, near = region_steps()
    base_counts = jax.random.randint(key, (PEERS, PEERS), 0, SLOTS + 1)
    busiest = jax.random.randint(jax.random.fold_in(key, 7), (), 0, PEERS)
    column = jnp.arange(PEERS)[None, :] == busiest
    filled = jnp.where(column, SLOTS, base_counts)
    return jnp.where(near, filled, 0).astype(jnp.int32)


def draw_import_shift(key, part):
    sky_step, depth_step, near = region_steps()
    across = jax.random.randint(key, (PEERS, PEERS, SLOTS), -1, 2)
    first = jnp.broadcast_to(sky_step[:, :, None], (PEERS, PEERS, SLOTS))
    third = jnp.broadcast_to(depth_step[:, :, None], (PEERS, PEERS, SLOTS))
    stacked = jnp.stack([first, across, third], axis=0)
    return jnp.where(near[None, :, :, None], stacked, 0).astype(jnp.int32)


def plant(values, rng, smallest, high):
    index_at = [jax.random.randint(jax.random.fold_in(rng, axis), (), 0, length) for axis, length in enumerate(values.shape)]
    widest = values.shape.index(max(values.shape))
    beside = index_at[:widest] + [(index_at[widest] + 1) % values.shape[widest]] + index_at[widest + 1:]
    return values.at[tuple(index_at)].set(smallest).at[tuple(beside)].set(high)


def levels(own_key, shape, cuts, smallest, high):
    gain = 1.0
    for position, blocks in cuts:
        heights = jax.random.uniform(jax.random.fold_in(jax.random.fold_in(own_key, 6), position), (blocks,), jnp.float32, smallest / len(cuts), high / len(cuts))
        gain = gain * jnp.repeat(jnp.exp(heights), shape[position] // blocks).reshape((-1,) + (1,) * (len(shape) - 1 - position))
    return gain


def setup_inputs(seed: int = 0) -> dict:
    key_list = jax.random.split(jax.random.key(seed), 8)
    positions = jnp.clip(1.0 * jax.random.uniform(key_list[0], (3, CELLS, PTS), jnp.float32) ** levels(key_list[0], (3, CELLS, PTS), ((1, 128),), -0.2, 0.2), 0.0, 1.0)
    cell_points = plant(jax.random.randint(key_list[1], (CELLS,), 1, PTS + 1), jax.random.fold_in(key_list[1], 1), 1, PTS).astype(jnp.int32)
    target_log = jnp.clip(jax.random.uniform(key_list[2], (BINS,), jnp.float32, 8.0, 20.0), 8.0, 20.0)
    export_count = draw_export_count(jax.random.fold_in(key_list[7], 71), 0)
    export_cell = plant(jax.random.randint(key_list[4], (PEERS, PEERS, SLOTS), 0, CELL_DEV), jax.random.fold_in(key_list[4], 1), 0, CELL_DEV - 1).astype(jnp.int32)
    import_pair = plant(jax.random.randint(key_list[5], (PEERS, PEERS, SLOTS), 0, CELL_DEV), jax.random.fold_in(key_list[5], 1), 0, CELL_DEV - 1).astype(jnp.int32)
    import_shift = draw_import_shift(jax.random.fold_in(key_list[7], 71), 0)
    return dict(positions=positions, cell_points=cell_points, target_log=target_log, export_count=export_count, export_cell=export_cell, import_pair=import_pair, import_shift=import_shift)


EPS_SQ = 0.0001
INV_WIDTH = 16.0
STEP_SIZE = 0.01

def pair_geometry(left_pos, left_mask, right_pos, right_mask, shifts, centres):
    offsets = left_pos[:, :, :, None] - right_pos[:, :, None, :] - shifts[:, :, None, None]
    radius = jnp.sqrt(lax.optimization_barrier(jnp.sum(offsets * offsets, axis=0)) + EPS_SQ)
    weight = left_mask[:, :, None] * right_mask[:, None, :]
    scaled = (radius[None] - centres[:, None, None, None]) * INV_WIDTH
    kernel = jnp.exp(-0.5 * scaled * scaled)
    return (offsets, radius, weight, scaled, kernel)

def block_counts(left_pos, left_mask, right_pos, right_mask, shifts, centres):
    offsets, radius, weight, scaled, kernel = pair_geometry(left_pos, left_mask, right_pos, right_mask, shifts, centres)
    return lax.optimization_barrier(jnp.sum(weight[None] * kernel, axis=(1, 2, 3)))

def block_forces(left_pos, left_mask, right_pos, right_mask, shifts, centres, bin_pull):
    offsets, radius, weight, scaled, kernel = pair_geometry(left_pos, left_mask, right_pos, right_mask, shifts, centres)
    slopes = lax.optimization_barrier(jnp.sum(bin_pull[:, None, None, None] * scaled * kernel, axis=0)) * -INV_WIDTH
    strength = weight * slopes / radius
    pulled = strength[None] * offsets
    return (lax.optimization_barrier(jnp.sum(pulled, axis=3)), -lax.optimization_barrier(jnp.sum(pulled, axis=2)))

def reference(positions, cell_points, target_log, export_count, export_cell, import_pair, import_shift):
    centres = (jnp.arange(BINS, dtype=jnp.float32) + 0.5) / INV_WIDTH
    point_mask = (jnp.arange(PTS, dtype=jnp.int32)[None, :] < cell_points[:, None]).astype(jnp.float32)
    dest_ids = jnp.broadcast_to(jnp.arange(PEERS, dtype=jnp.int32)[:, None, None], (PEERS, PEERS, SLOTS))
    source_ids = jnp.broadcast_to(jnp.arange(PEERS, dtype=jnp.int32)[None, :, None], (PEERS, PEERS, SLOTS))
    slot_ids = jnp.broadcast_to(jnp.arange(SLOTS, dtype=jnp.int32)[None, None, :], (PEERS, PEERS, SLOTS))
    sent_cells = jnp.transpose(export_cell, (1, 0, 2))
    sent_counts = jnp.transpose(export_count, (1, 0))[:, :, None]
    live_pairs = (slot_ids < sent_counts).astype(jnp.float32)
    block_rows = 64
    block_total = PEERS * PEERS * SLOTS // block_rows
    left_cells = (dest_ids * CELL_DEV + import_pair).astype(jnp.int32).reshape(block_total, block_rows)
    right_cells = (source_ids * CELL_DEV + sent_cells).astype(jnp.int32).reshape(block_total, block_rows)
    live_flat = live_pairs.reshape(block_total, block_rows)
    shift_flat = jnp.moveaxis(import_shift.astype(jnp.float32).reshape(3, block_total, block_rows), 1, 0)
    self_mask = point_mask.reshape(PEERS, CELL_DEV, PTS)
    zero_shift = jnp.zeros((3, CELL_DEV), jnp.float32)
    coords = positions
    travel = jnp.zeros_like(positions)
    for iteration in range(STEPS):
        self_pos = jnp.moveaxis(coords.reshape(3, PEERS, CELL_DEV, PTS), 1, 0)

        def self_count(running, item):
            cell_pos, cell_mask = item
            return (running + block_counts(cell_pos, cell_mask, cell_pos, cell_mask, zero_shift, centres), None)
        self_total, _ = lax.scan(self_count, jnp.zeros((BINS,), jnp.float32), (self_pos, self_mask))

        def ghost_count(running, item):
            left_ids, right_ids, live_now, shift_now = item
            part_sum = block_counts(coords[:, left_ids], point_mask[left_ids], coords[:, right_ids], point_mask[right_ids] * live_now[:, None], shift_now, centres)
            return (running + part_sum, None)
        ghost_total, _ = lax.scan(ghost_count, jnp.zeros((BINS,), jnp.float32), (left_cells, right_cells, live_flat, shift_flat))
        counts = 0.5 * self_total + ghost_total
        mean_count = jnp.mean(counts)
        bin_pull = (jnp.log(1.0 + counts) - target_log) * mean_count / (1.0 + counts)

        def self_force(item):
            cell_pos, cell_mask = item
            force_left, force_right = block_forces(cell_pos, cell_mask, cell_pos, cell_mask, zero_shift, centres, bin_pull)
            return force_left
        self_grad = lax.map(self_force, (self_pos, self_mask))
        gradient = jnp.moveaxis(self_grad, 0, 1).reshape(3, CELLS, PTS)

        def ghost_force(running, item):
            left_ids, right_ids, live_now, shift_now = item
            force_left, force_right = block_forces(coords[:, left_ids], point_mask[left_ids], coords[:, right_ids], point_mask[right_ids] * live_now[:, None], shift_now, centres, bin_pull)
            running = running.at[:, left_ids].add(force_left)
            running = running.at[:, right_ids].add(force_right)
            return (running, None)
        gradient, _ = lax.scan(ghost_force, gradient, (left_cells, right_cells, live_flat, shift_flat))
        power_sum = jnp.sum(gradient * gradient)
        valid_count = jnp.sum(point_mask)
        grad_rms = jnp.sqrt(power_sum / (3.0 * valid_count) + 1e-06)
        move_dir = -gradient / grad_rms
        travel = travel + move_dir
        coords = coords + STEP_SIZE * move_dir
    return travel
```

```python
import functools
import math

import jax
import jax.numpy as jnp
from jax import lax
from jax.experimental import pallas as pl
from jax.experimental.pallas import tpu as pltpu
from jax.sharding import PartitionSpec as P

STEPS = 2
EPS_SQ = 0.0001
STEP_SIZE = 0.01

BINS = 16
CELLS = 16
POINTS = 128
SLOTS = 3
AXES = ("sky", "depth")

UNIT = math.sqrt(128.0 * math.log2(math.e))
CENTRES = [(b + 0.5) / 16.0 for b in range(BINS)]
CHAIN = 4
LIFT = 64.0
MIDDLE = CENTRES[8]
RADIUS_CAP = 2.1 * UNIT
FAR = 1.0e4
COUNT_SCALE = [
    math.exp(16.0 * (b % CHAIN) * (MIDDLE - CENTRES[b - b % CHAIN]) - 0.5 * (b % CHAIN) ** 2) * 2.0**-LIFT
    for b in range(BINS)
]
FORCE_SCALE = [-256.0 / UNIT * scale for scale in COUNT_SCALE]

NEIGHBOURS = [(0, -1), (0, 1), (-1, 0), (-1, -1), (-1, 1), (1, 0), (1, -1), (1, 1)]
N_JOBS = 8 * SLOTS
STEP_ROWS = 16

VMEM = pl.BlockSpec(memory_space=pltpu.VMEM)
SMEM = pl.BlockSpec(memory_space=pltpu.SMEM)
PARAMS = pltpu.CompilerParams(vmem_limit_bytes=40 * 1024 * 1024)


def neighbour(across, along):
    sky_count, depth_count = lax.axis_size("sky"), lax.axis_size("depth")
    sky = lax.rem(lax.axis_index("sky") + (across + sky_count), sky_count)
    depth = lax.axis_index("depth") + along
    inside = (depth >= 0) & (depth < depth_count)
    return sky * depth_count + jnp.clip(depth, 0, depth_count - 1), inside


def column(values, shape):
    rows = lax.broadcasted_iota(jnp.int32, shape, 0)
    out = jnp.full(shape, values[0], jnp.float32)
    for index in range(1, len(values)):
        out = jnp.where(rows == index, values[index], out)
    return out


def pack(source, points, export_count, export_cell, import_pair, import_shift, outs):
    depth_up, depth_down, sky_up, sky_down = outs
    lanes = lax.broadcasted_iota(jnp.int32, (4, POINTS), 1)
    rows = lax.broadcasted_iota(jnp.int32, (4, POINTS), 0)
    for across in (-1, 0, 1):
        for along in (-1, 0, 1):
            if (across, along) == (0, 0):
                continue
            if along == 1:
                out = depth_up.at[across + 1]
            elif along == -1:
                out = depth_down.at[across + 1]
            else:
                out = sky_up if across == 1 else sky_down
            device, inside = neighbour(across, along)
            live = jnp.where(inside, export_count[0, device], 0)
            meta = jnp.zeros((4, POINTS), jnp.float32)
            for slot in range(SLOTS):
                right = export_cell[slot, device]
                out[slot] = source[right]
                size = jnp.where(slot < live, points[right], 0)
                meta = jnp.where(lanes == slot, size.astype(jnp.float32), meta)
                left = import_pair[slot, device]
                shift = jnp.zeros((4, POINTS), jnp.float32)
                for axis in range(3):
                    amount = import_shift[axis * SLOTS + slot, device].astype(jnp.float32) * UNIT
                    shift = jnp.where(rows == axis, amount, shift)
                out[SLOTS + slot] = source[left] - shift
                meta = jnp.where(lanes == SLOTS + slot, points[left].astype(jnp.float32), meta)
            out[2 * SLOTS] = meta


def first_kernel(
    positions, points, export_count, export_cell, import_pair, import_shift,
    target, depth_up, depth_down, sky_up, sky_down, source,
):
    lanes = lax.broadcasted_iota(jnp.int32, (4, POINTS), 1)
    for cell in range(CELLS):
        rows = [positions[axis, cell : cell + 1, :] for axis in range(3)]
        tile = jnp.concatenate(rows + [jnp.zeros((1, POINTS), jnp.float32)], axis=0) * UNIT
        live = lanes < points[cell]
        target[cell] = jnp.where(live, tile, -FAR)
        source[cell] = jnp.where(live, tile, FAR)
    pack(
        source, points, export_count, export_cell, import_pair, import_shift,
        (depth_up, depth_down, sky_up, sky_down),
    )


def add_pairs(job, slot, cell, size, target, source, force, counts):
    target_x = jnp.broadcast_to(target[cell, 0:1, :], (STEP_ROWS, POINTS))
    target_y = jnp.broadcast_to(target[cell, 1:2, :], (STEP_ROWS, POINTS))
    target_z = jnp.broadcast_to(target[cell, 2:3, :], (STEP_ROWS, POINTS))

    def step(index, unused):
        block = source[slot, pl.ds(pl.multiple_of(index * STEP_ROWS, STEP_ROWS), STEP_ROWS), :]
        dx = target_x - block[:, 0:1]
        dy = target_y - block[:, 1:2]
        dz = target_z - block[:, 2:3]
        square = dx * dx + dy * dy + dz * dz + EPS_SQ * UNIT * UNIT
        inverse = lax.rsqrt(square)
        radius = jnp.minimum(square * inverse, RADIUS_CAP)
        units = (dx * inverse, dy * inverse, dz * inverse)
        ratio = jnp.exp2(
            radius * (16.0 * math.log2(math.e) / UNIT) - 16.0 * math.log2(math.e) * MIDDLE
        )
        for chain in range(BINS // CHAIN):
            for link in range(CHAIN):
                b = chain * CHAIN + link
                delta = radius - CENTRES[b] * UNIT
                if link == 0:
                    value = jnp.exp2(LIFT - delta * delta)
                else:
                    value = value * ratio
                if counts is not None:
                    counts[b] += value[:8] + value[8:]
                slope = value * delta
                for axis in range(3):
                    pulled = slope * units[axis]
                    force[cell, axis * BINS + b] += pulled[:8] + pulled[8:]
        return unused

    lax.fori_loop(0, (size + (STEP_ROWS - 1)) // STEP_ROWS, step, 0)


def pair_kernel(
    target, points, export_count, export_cell, import_pair, import_shift,
    from_below, from_above, from_left, from_right,
    grad, payload, source, force, self_counts, pair_counts, meta, sems,
):
    lanes = lax.broadcasted_iota(jnp.int32, (4, POINTS), 1)
    rows = lax.broadcasted_iota(jnp.int32, (4, POINTS), 0)
    messages = [
        from_below.at[1], from_above.at[1],
        from_left.at[0], from_left.at[1], from_left.at[2],
        from_right.at[0], from_right.at[1], from_right.at[2],
    ]
    copies = [
        pltpu.make_async_copy(message.at[2 * SLOTS], meta.at[index], sems.at[index])
        for index, message in enumerate(messages)
    ]
    for copy in copies:
        copy.start()
    force[...] = jnp.zeros(force.shape, jnp.float32)
    self_counts[...] = jnp.zeros(self_counts.shape, jnp.float32)
    pair_counts[...] = jnp.zeros(pair_counts.shape, jnp.float32)

    def put(slot, tile):
        source[slot] = jnp.transpose(jnp.concatenate([tile, tile], axis=0), (1, 0))

    for cell in range(CELLS):
        put(cell, jnp.where(lanes < points[cell], target[cell], FAR))
    for index, (across, along) in enumerate(NEIGHBOURS):
        device, inside = neighbour(across, along)
        for slot in range(SLOTS):
            shift = jnp.zeros((4, POINTS), jnp.float32)
            for axis in range(3):
                amount = import_shift[axis * SLOTS + slot, device].astype(jnp.float32) * UNIT
                shift = jnp.where(rows == axis, amount, shift)
            put(CELLS + index * SLOTS + slot, messages[index][slot] + shift)
            put(CELLS + N_JOBS + index * SLOTS + slot, messages[index][SLOTS + slot])
    for copy in copies:
        copy.wait()

    def self_job(job, unused):
        add_pairs(job, job, job, points[job], target, source, force, self_counts)
        return unused

    lax.fori_loop(0, CELLS, self_job, 0)

    for index, (across, along) in enumerate(NEIGHBOURS):
        device, inside = neighbour(across, along)
        live = jnp.where(inside, export_count[0, device], 0)

        def import_job(slot, unused, index=index, device=device):
            size = meta[index, 0, slot].astype(jnp.int32)
            add_pairs(
                slot, CELLS + index * SLOTS + slot, import_pair[slot, device], size,
                target, source, force, pair_counts,
            )
            return unused

        def export_job(slot, unused, index=index, device=device, live=live):
            size = meta[index, 0, SLOTS + slot].astype(jnp.int32)
            add_pairs(
                slot, CELLS + N_JOBS + index * SLOTS + slot, export_cell[slot, device], size,
                target, source, force, None,
            )
            return unused

        lax.fori_loop(0, SLOTS, import_job, 0)
        lax.fori_loop(0, live, export_job, 0)

    force_scale = column(FORCE_SCALE, (BINS, POINTS))
    for cell in range(CELLS):
        for axis in range(3):
            tile = jnp.sum(force[cell, axis * BINS : (axis + 1) * BINS], axis=1) * force_scale
            at = (cell * 3 + axis) * POINTS
            grad[:, at : at + POINTS] = tile
    whole = grad[...]
    gram = lax.dot_general(
        whole, whole, (((1,), (1,)), ((), ())),
        precision=lax.Precision.HIGHEST, preferred_element_type=jnp.float32,
    )
    bins = lax.broadcasted_iota(jnp.int32, (BINS, POINTS), 0)
    lane = lax.broadcasted_iota(jnp.int32, (BINS, POINTS), 1)
    low, high = lane % BINS, lane // BINS
    spread = jnp.where(low == bins, 1.0, 0.0)
    wide = lax.dot_general(
        gram, spread, (((1,), (0,)), ((), ())),
        precision=lax.Precision.HIGHEST, preferred_element_type=jnp.float32,
    )
    first = jnp.sum(jnp.where(bins == (low + high) % BINS, wide, 0.0), axis=0, keepdims=True)
    second = jnp.where((bins == (low + 8) % BINS) & (high == 0), wide, 0.0)
    sums = jnp.sum(0.5 * self_counts[...] + pair_counts[...], axis=1)
    sums = jnp.sum(sums, axis=1, keepdims=True) * column(COUNT_SCALE, (BINS, POINTS))
    second = second + jnp.where(lane == bins + BINS, sums, 0.0)
    total = points[0]
    for cell in range(1, CELLS):
        total = total + points[cell]
    second = second + jnp.where((lane == 2 * BINS) & (bins == 0), total.astype(jnp.float32), 0.0)
    second = jnp.sum(second, axis=0, keepdims=True)
    both = jnp.concatenate([first, second], axis=0)
    payload[...] = jnp.broadcast_to(both[None], payload.shape)


def moves_of(sums, grad, target_log):
    both = jnp.sum(sums[...], axis=0)
    bins = lax.broadcasted_iota(jnp.int32, (BINS, POINTS), 0)
    lane = lax.broadcasted_iota(jnp.int32, (BINS, POINTS), 1)
    low, high = lane % BINS, lane // BINS
    first, second = both[0:1], both[1:2]
    counts = jnp.sum(
        jnp.where(lane == bins + BINS, jnp.broadcast_to(second, (BINS, POINTS)), 0.0), axis=1, keepdims=True
    )
    counts = jnp.broadcast_to(counts, (BINS, POINTS))
    one_lane = lax.broadcasted_iota(jnp.int32, (1, POINTS), 1)
    valid = jnp.sum(jnp.where(one_lane == 2 * BINS, second, 0.0), axis=1, keepdims=True)
    mean_count = jnp.sum(counts, axis=0, keepdims=True) / BINS
    logs = column([target_log[b] for b in range(BINS)], (BINS, POINTS))
    pull = (jnp.log(1.0 + counts) - logs) * mean_count / (1.0 + counts)
    here = jnp.sum(jnp.where(bins == low, pull, 0.0), axis=0, keepdims=True)
    there = jnp.sum(jnp.where(bins == (low + high) % BINS, pull, 0.0), axis=0, keepdims=True)
    across = jnp.sum(jnp.where(bins == (low + 8) % BINS, pull, 0.0), axis=0, keepdims=True)
    power = first * here * there * jnp.where(one_lane < BINS, 1.0, 2.0)
    power = power + jnp.where(one_lane < BINS, second * here * across, 0.0)
    power = jnp.maximum(jnp.sum(power, axis=1, keepdims=True), 0.0)
    rms = jnp.sqrt(power / (3.0 * valid) + 1e-06)
    weights = pull / -rms
    out = []
    for cell in range(CELLS):
        parts = []
        for axis in range(3):
            at = (cell * 3 + axis) * POINTS
            parts.append(jnp.sum(grad[:, at : at + POINTS] * weights, axis=0, keepdims=True))
        out.append(parts)
    return out


def update_kernel(
    sums, grad, target, target_log, points, export_count, export_cell, import_pair, import_shift,
    travel, next_target, depth_up, depth_down, sky_up, sky_down, source,
):
    lanes = lax.broadcasted_iota(jnp.int32, (4, POINTS), 1)
    moves = moves_of(sums, grad, target_log)
    for cell in range(CELLS):
        tile = jnp.concatenate(moves[cell] + [jnp.zeros((1, POINTS), jnp.float32)], axis=0)
        travel[cell] = tile
        tile = target[cell] + (STEP_SIZE * UNIT) * tile
        next_target[cell] = tile
        source[cell] = jnp.where(lanes < points[cell], tile, FAR)
    pack(
        source, points, export_count, export_cell, import_pair, import_shift,
        (depth_up, depth_down, sky_up, sky_down),
    )


def last_kernel(sums, grad, travel, target_log, out):
    moves = moves_of(sums, grad, target_log)
    for cell in range(CELLS):
        for axis in range(3):
            out[axis, cell : cell + 1, :] = travel[cell, axis : axis + 1, :] + moves[cell][axis]


def f32(*shape):
    return jax.ShapeDtypeStruct(shape, jnp.float32)


CELL_SHAPE = (CELLS, 4, POINTS)
GRAD_SHAPE = (BINS, CELLS * 3 * POINTS)
MESSAGE = (2 * SLOTS + 1, 4, POINTS)
MESSAGES = [f32(3, *MESSAGE), f32(3, *MESSAGE), f32(*MESSAGE), f32(*MESSAGE)]


def along_depth(value, by):
    count = lax.axis_size("depth")
    return lax.ppermute(value, "depth", [(i, i + by) for i in range(count) if 0 <= i + by < count])


def along_sky(value, by):
    count = lax.axis_size("sky")
    return lax.ppermute(value, "sky", [(i, (i + by) % count) for i in range(count)])


def body(positions, cell_points, target_log, export_count, export_cell, import_pair, import_shift):
    devices = export_count.shape[1]
    tables = (
        cell_points,
        export_count,
        jnp.transpose(export_cell[0], (1, 0)),
        jnp.transpose(import_pair[0], (1, 0)),
        jnp.transpose(import_shift[:, 0], (0, 2, 1)).reshape(3 * SLOTS, devices),
    )
    target, *messages = pl.pallas_call(
        first_kernel,
        out_shape=[f32(*CELL_SHAPE)] + MESSAGES,
        in_specs=[VMEM] + [SMEM] * 5,
        out_specs=[VMEM] * 5,
        scratch_shapes=[pltpu.VMEM(CELL_SHAPE, jnp.float32)],
        compiler_params=PARAMS,
        name="first",
    )(positions, *tables)
    for iteration in range(STEPS):
        depth_up, depth_down, sky_up, sky_down = messages
        from_below = along_depth(depth_up, 1)
        from_above = along_depth(depth_down, -1)
        from_left = along_sky(jnp.stack([sky_up, from_below[2], from_above[2]]), 1)
        from_right = along_sky(jnp.stack([sky_down, from_below[0], from_above[0]]), -1)
        grad, payload = pl.pallas_call(
            pair_kernel,
            out_shape=[f32(*GRAD_SHAPE), f32(devices, 2, POINTS)],
            in_specs=[VMEM] + [SMEM] * 5 + [VMEM] * 4,
            out_specs=[VMEM] * 2,
            scratch_shapes=[
                pltpu.VMEM((CELLS + 2 * N_JOBS, POINTS, 8), jnp.float32),
                pltpu.VMEM((CELLS, 3 * BINS, 8, POINTS), jnp.float32),
                pltpu.VMEM((BINS, 8, POINTS), jnp.float32),
                pltpu.VMEM((BINS, 8, POINTS), jnp.float32),
                pltpu.SMEM((8, 4, POINTS), jnp.float32),
                pltpu.SemaphoreType.DMA((8,)),
            ],
            compiler_params=PARAMS,
            name="pairs",
        )(target, *tables, from_below, from_above, from_left, from_right)
        sums = lax.all_to_all(payload, AXES, 0, 0)
        if iteration == STEPS - 1:
            return pl.pallas_call(
                last_kernel,
                out_shape=f32(*positions.shape),
                in_specs=[VMEM] * 3 + [SMEM],
                out_specs=VMEM,
                compiler_params=PARAMS,
                name="last",
            )(sums, grad, travel, target_log)
        travel, target, *messages = pl.pallas_call(
            update_kernel,
            out_shape=[f32(*CELL_SHAPE), f32(*CELL_SHAPE)] + MESSAGES,
            in_specs=[VMEM] * 3 + [SMEM] * 6,
            out_specs=[VMEM] * 6,
            scratch_shapes=[pltpu.VMEM(CELL_SHAPE, jnp.float32)],
            compiler_params=PARAMS,
            name="update",
        )(sums, grad, target, target_log, *tables)


def solution(mesh):
    in_specs = (
        P(None, ("sky", "depth"), None),
        P(("sky", "depth")),
        P(),
        P(("sky", "depth"), None),
        P(("sky", "depth"), None, None),
        P(("sky", "depth"), None, None),
        P(None, ("sky", "depth"), None, None),
    )
    out_specs = P(None, ("sky", "depth"), None)
    return jax.shard_map(body, mesh=mesh, in_specs=in_specs, out_specs=out_specs, check_vma=False)
```

```python
import functools
import math

import jax
import jax.numpy as jnp
from jax import lax
from jax.experimental import pallas as pl
from jax.experimental.pallas import tpu as pltpu
from jax.sharding import PartitionSpec as P

STEPS = 2
EPS_SQ = 0.0001
STEP_SIZE = 0.01

BINS = 16
CELLS = 16
POINTS = 128
SLOTS = 3
AXES = ("sky", "depth")

UNIT = math.sqrt(128.0 * math.log2(math.e))
CENTRES = [(b + 0.5) / 16.0 for b in range(BINS)]
CHAIN = 4
LIFT = 64.0
MIDDLE = CENTRES[8]
RADIUS_CAP = 2.1 * UNIT
FAR = 1.0e4
COUNT_SCALE = [
    math.exp(16.0 * (b % CHAIN) * (MIDDLE - CENTRES[b - b % CHAIN]) - 0.5 * (b % CHAIN) ** 2) * 2.0**-LIFT
    for b in range(BINS)
]
FORCE_SCALE = [-256.0 / UNIT * scale for scale in COUNT_SCALE]

NEIGHBOURS = [(0, -1), (0, 1), (-1, 0), (-1, -1), (-1, 1), (1, 0), (1, -1), (1, 1)]
STEP_ROWS = 16
BLOCKS = POINTS // STEP_ROWS
UNROLL = 2

VMEM = pl.BlockSpec(memory_space=pltpu.VMEM)
SMEM = pl.BlockSpec(memory_space=pltpu.SMEM)
PARAMS = pltpu.CompilerParams(vmem_limit_bytes=40 * 1024 * 1024)


def neighbour(across, along):
    sky_count, depth_count = lax.axis_size("sky"), lax.axis_size("depth")
    sky = lax.rem(lax.axis_index("sky") + (across + sky_count), sky_count)
    depth = lax.axis_index("depth") + along
    inside = (depth >= 0) & (depth < depth_count)
    return sky * depth_count + jnp.clip(depth, 0, depth_count - 1), inside


def column(values, shape):
    rows = lax.broadcasted_iota(jnp.int32, shape, 0)
    out = jnp.full(shape, values[0], jnp.float32)
    for index in range(1, len(values)):
        out = jnp.where(rows == index, values[index], out)
    return out


def pack(source, points, export_count, export_cell, import_pair, import_shift, outs):
    depth_up, depth_down, sky_up, sky_down = outs
    lanes = lax.broadcasted_iota(jnp.int32, (4, POINTS), 1)
    rows = lax.broadcasted_iota(jnp.int32, (4, POINTS), 0)
    for across in (-1, 0, 1):
        for along in (-1, 0, 1):
            if (across, along) == (0, 0):
                continue
            if along == 1:
                out = depth_up.at[across + 1]
            elif along == -1:
                out = depth_down.at[across + 1]
            else:
                out = sky_up if across == 1 else sky_down
            device, inside = neighbour(across, along)
            live = jnp.where(inside, export_count[0, device], 0)
            meta = jnp.zeros((4, POINTS), jnp.float32)
            for slot in range(SLOTS):
                right = export_cell[slot, device]
                out[slot] = source[right]
                size = jnp.where(slot < live, points[right], 0)
                meta = jnp.where(lanes == slot, size.astype(jnp.float32), meta)
                left = import_pair[slot, device]
                shift = jnp.zeros((4, POINTS), jnp.float32)
                for axis in range(3):
                    amount = import_shift[axis * SLOTS + slot, device].astype(jnp.float32) * UNIT
                    shift = jnp.where(rows == axis, amount, shift)
                out[SLOTS + slot] = source[left] - shift
                meta = jnp.where(lanes == SLOTS + slot, points[left].astype(jnp.float32), meta)
            out[2 * SLOTS] = meta


def first_kernel(
    positions, points, export_count, export_cell, import_pair, import_shift,
    target, depth_up, depth_down, sky_up, sky_down, source,
):
    lanes = lax.broadcasted_iota(jnp.int32, (4, POINTS), 1)
    for cell in range(CELLS):
        rows = [positions[axis, cell : cell + 1, :] for axis in range(3)]
        tile = jnp.concatenate(rows + [jnp.zeros((1, POINTS), jnp.float32)], axis=0) * UNIT
        live = lanes < points[cell]
        target[cell] = jnp.where(live, tile, -FAR)
        source[cell] = jnp.where(live, tile, FAR)
    pack(
        source, points, export_count, export_cell, import_pair, import_shift,
        (depth_up, depth_down, sky_up, sky_down),
    )


def spread_points(at, row_list, source, base, spread):
    blocks = [
        source[pl.ds(pl.multiple_of(row_list[at + unit] * STEP_ROWS, STEP_ROWS), STEP_ROWS), :]
        for unit in range(UNROLL)
    ]
    for axis in range(3):
        for unit in range(UNROLL):
            lane = base + axis
            spread[unit, axis] = jnp.broadcast_to(blocks[unit][:, lane : lane + 1], (STEP_ROWS, POINTS))


def shape_pairs(at, cell_list, target, spread, shapes):
    for unit in range(UNROLL):
        cell = cell_list[at + unit]
        dx, dy, dz = (target[cell, axis : axis + 1, :] - spread[unit, axis] for axis in range(3))
        square = dx * dx + dy * dy + dz * dz + EPS_SQ * UNIT * UNIT
        inverse = lax.rsqrt(square)
        radius = jnp.minimum(square * inverse, RADIUS_CAP)
        ratio = jnp.exp2(
            radius * (16.0 * math.log2(math.e) / UNIT) - 16.0 * math.log2(math.e) * MIDDLE
        )
        for index, value in enumerate((radius, ratio, dx * inverse, dy * inverse, dz * inverse)):
            shapes[unit, index] = value


def add_block(values, cell, force, counts):
    radius, ratio, *units = values
    for chain in range(BINS // CHAIN):
        for link in range(CHAIN):
            b = chain * CHAIN + link
            delta = radius - CENTRES[b] * UNIT
            if link == 0:
                value = jnp.exp2(LIFT - delta * delta)
            else:
                value = value * ratio
            if counts is not None:
                counts[b] += value[:8] + value[8:]
            slope = value * delta
            for axis in range(3):
                pulled = slope * units[axis]
                force[cell, axis * BINS + b] += pulled[:8] + pulled[8:]


def add_blocks(total, row_list, cell_list, base, target, source, force, counts, spread, shapes):
    spread_points(0, row_list, source, base, spread)
    shape_pairs(0, cell_list, target, spread, shapes)
    spread_points(UNROLL, row_list, source, base, spread)

    def step(turn, unused):
        at = turn * UNROLL
        now = [[shapes[unit, index] for index in range(5)] for unit in range(UNROLL)]
        shape_pairs(at + UNROLL, cell_list, target, spread, shapes)
        spread_points(at + 2 * UNROLL, row_list, source, base, spread)
        for unit in range(UNROLL):
            add_block(now[unit], cell_list[at + unit], force, counts)
        return unused

    lax.fori_loop(0, (total + (UNROLL - 1)) // UNROLL, step, 0)


def list_blocks(at, slot, cell, size, row_list, cell_list):
    for block in range(BLOCKS):
        row_list[at + block] = slot * BLOCKS + block
        cell_list[at + block] = cell
    return at + (size + (STEP_ROWS - 1)) // STEP_ROWS


def end_list(at, slots, row_list, cell_list):
    for spare in range(3 * UNROLL):
        row_list[at + spare] = slots * BLOCKS
        cell_list[at + spare] = 0


def put_points(source, slot, first, second):
    source[slot * POINTS : (slot + 1) * POINTS] = jnp.transpose(
        jnp.concatenate([first, second], axis=0), (1, 0)
    )


def self_kernel(target, points, force, counts, source, row_list, cell_list, spread, shapes):
    lanes = lax.broadcasted_iota(jnp.int32, (4, POINTS), 1)
    end = 0
    for cell in range(CELLS):
        tile = jnp.where(lanes < points[cell], target[cell], FAR)
        put_points(source, cell, tile, tile)
        end = list_blocks(end, cell, cell, points[cell], row_list, cell_list)
    end_list(end, CELLS, row_list, cell_list)
    source[CELLS * POINTS :] = jnp.full((STEP_ROWS, 8), FAR, jnp.float32)
    force[...] = jnp.zeros(force.shape, jnp.float32)
    counts[...] = jnp.zeros(counts.shape, jnp.float32)
    add_blocks(end, row_list, cell_list, 0, target, source, force, counts, spread, shapes)
    counts[...] = 0.5 * counts[...]


def ghost_pairs(
    messages, neighbours, target, export_count, export_cell, import_pair, import_shift, force, counts,
    source, import_rows, import_cells, export_rows, export_cells, meta, sems, spread, shapes,
):
    rows = lax.broadcasted_iota(jnp.int32, (4, POINTS), 0)
    copies = [
        pltpu.make_async_copy(message.at[2 * SLOTS], meta.at[index], sems.at[index])
        for index, message in enumerate(messages)
    ]
    for copy in copies:
        copy.start()
    for index, (across, along) in enumerate(neighbours):
        device, inside = neighbour(across, along)
        for slot in range(SLOTS):
            shift = jnp.zeros((4, POINTS), jnp.float32)
            for axis in range(3):
                amount = import_shift[axis * SLOTS + slot, device].astype(jnp.float32) * UNIT
                shift = jnp.where(rows == axis, amount, shift)
            put_points(source, index * SLOTS + slot, messages[index][slot] + shift, messages[index][SLOTS + slot])
    slots = len(neighbours) * SLOTS
    source[slots * POINTS :] = jnp.full((STEP_ROWS, 8), FAR, jnp.float32)
    for copy in copies:
        copy.wait()
    import_end = 0
    export_end = 0
    for index, (across, along) in enumerate(neighbours):
        device, inside = neighbour(across, along)
        live = jnp.where(inside, export_count[0, device], 0)
        for slot in range(SLOTS):
            at = index * SLOTS + slot
            size = meta[index, 0, slot].astype(jnp.int32)
            import_end = list_blocks(
                import_end, at, import_pair[slot, device], size, import_rows, import_cells
            )
            size = jnp.where(slot < live, meta[index, 0, SLOTS + slot].astype(jnp.int32), 0)
            export_end = list_blocks(
                export_end, at, export_cell[slot, device], size, export_rows, export_cells
            )
    end_list(import_end, slots, import_rows, import_cells)
    end_list(export_end, slots, export_rows, export_cells)
    add_blocks(
        import_end, import_rows, import_cells, 0, target, source, force, counts, spread, shapes
    )
    add_blocks(
        export_end, export_rows, export_cells, 4, target, source, force, None, spread, shapes
    )


def near_kernel(
    target, export_count, export_cell, import_pair, import_shift, from_below, from_above,
    force_in, counts_in, force, counts, *scratch,
):
    ghost_pairs(
        [from_below.at[1], from_above.at[1]], NEIGHBOURS[:2],
        target, export_count, export_cell, import_pair, import_shift, force, counts, *scratch,
    )


def far_kernel(
    target, points, export_count, export_cell, import_pair, import_shift, from_left, from_right,
    force_in, counts_in, force, counts, grad, payload, *scratch,
):
    ghost_pairs(
        [side.at[index] for side in (from_left, from_right) for index in range(3)], NEIGHBOURS[2:],
        target, export_count, export_cell, import_pair, import_shift, force, counts, *scratch,
    )
    force_scale = column(FORCE_SCALE, (BINS, POINTS))
    for cell in range(CELLS):
        for axis in range(3):
            tile = jnp.sum(force[cell, axis * BINS : (axis + 1) * BINS], axis=1) * force_scale
            at = (cell * 3 + axis) * POINTS
            grad[:, at : at + POINTS] = tile
    whole = grad[...]
    gram = lax.dot_general(
        whole, whole, (((1,), (1,)), ((), ())),
        precision=lax.Precision.HIGHEST, preferred_element_type=jnp.float32,
    )
    bins = lax.broadcasted_iota(jnp.int32, (BINS, POINTS), 0)
    lane = lax.broadcasted_iota(jnp.int32, (BINS, POINTS), 1)
    low, high = lane % BINS, lane // BINS
    spread = jnp.where(low == bins, 1.0, 0.0)
    wide = lax.dot_general(
        gram, spread, (((1,), (0,)), ((), ())),
        precision=lax.Precision.HIGHEST, preferred_element_type=jnp.float32,
    )
    first = jnp.sum(jnp.where(bins == (low + high) % BINS, wide, 0.0), axis=0, keepdims=True)
    second = jnp.where((bins == (low + 8) % BINS) & (high == 0), wide, 0.0)
    sums = jnp.sum(counts[...], axis=1)
    sums = jnp.sum(sums, axis=1, keepdims=True) * column(COUNT_SCALE, (BINS, POINTS))
    second = second + jnp.where(lane == bins + BINS, sums, 0.0)
    total = points[0]
    for cell in range(1, CELLS):
        total = total + points[cell]
    second = second + jnp.where((lane == 2 * BINS) & (bins == 0), total.astype(jnp.float32), 0.0)
    second = jnp.sum(second, axis=0, keepdims=True)
    both = jnp.concatenate([first, second], axis=0)
    payload[...] = jnp.broadcast_to(both[None], payload.shape)


def moves_of(sums, grad, target_log):
    both = jnp.sum(sums[...], axis=0)
    bins = lax.broadcasted_iota(jnp.int32, (BINS, POINTS), 0)
    lane = lax.broadcasted_iota(jnp.int32, (BINS, POINTS), 1)
    low, high = lane % BINS, lane // BINS
    first, second = both[0:1], both[1:2]
    counts = jnp.sum(
        jnp.where(lane == bins + BINS, jnp.broadcast_to(second, (BINS, POINTS)), 0.0), axis=1, keepdims=True
    )
    counts = jnp.broadcast_to(counts, (BINS, POINTS))
    one_lane = lax.broadcasted_iota(jnp.int32, (1, POINTS), 1)
    valid = jnp.sum(jnp.where(one_lane == 2 * BINS, second, 0.0), axis=1, keepdims=True)
    mean_count = jnp.sum(counts, axis=0, keepdims=True) / BINS
    logs = column([target_log[b] for b in range(BINS)], (BINS, POINTS))
    pull = (jnp.log(1.0 + counts) - logs) * mean_count / (1.0 + counts)
    here = jnp.sum(jnp.where(bins == low, pull, 0.0), axis=0, keepdims=True)
    there = jnp.sum(jnp.where(bins == (low + high) % BINS, pull, 0.0), axis=0, keepdims=True)
    across = jnp.sum(jnp.where(bins == (low + 8) % BINS, pull, 0.0), axis=0, keepdims=True)
    power = first * here * there * jnp.where(one_lane < BINS, 1.0, 2.0)
    power = power + jnp.where(one_lane < BINS, second * here * across, 0.0)
    power = jnp.maximum(jnp.sum(power, axis=1, keepdims=True), 0.0)
    rms = jnp.sqrt(power / (3.0 * valid) + 1e-06)
    weights = pull / -rms
    out = []
    for cell in range(CELLS):
        parts = []
        for axis in range(3):
            at = (cell * 3 + axis) * POINTS
            parts.append(jnp.sum(grad[:, at : at + POINTS] * weights, axis=0, keepdims=True))
        out.append(parts)
    return out


def update_kernel(
    sums, grad, target, target_log, points, export_count, export_cell, import_pair, import_shift,
    travel, next_target, depth_up, depth_down, sky_up, sky_down, source,
):
    lanes = lax.broadcasted_iota(jnp.int32, (4, POINTS), 1)
    moves = moves_of(sums, grad, target_log)
    for cell in range(CELLS):
        tile = jnp.concatenate(moves[cell] + [jnp.zeros((1, POINTS), jnp.float32)], axis=0)
        travel[cell] = tile
        tile = target[cell] + (STEP_SIZE * UNIT) * tile
        next_target[cell] = tile
        source[cell] = jnp.where(lanes < points[cell], tile, FAR)
    pack(
        source, points, export_count, export_cell, import_pair, import_shift,
        (depth_up, depth_down, sky_up, sky_down),
    )


def last_kernel(sums, grad, travel, target_log, out):
    moves = moves_of(sums, grad, target_log)
    for cell in range(CELLS):
        for axis in range(3):
            out[axis, cell : cell + 1, :] = travel[cell, axis : axis + 1, :] + moves[cell][axis]


def f32(*shape):
    return jax.ShapeDtypeStruct(shape, jnp.float32)


CELL_SHAPE = (CELLS, 4, POINTS)
GRAD_SHAPE = (BINS, CELLS * 3 * POINTS)
MESSAGE = (2 * SLOTS + 1, 4, POINTS)
MESSAGES = [f32(3, *MESSAGE), f32(3, *MESSAGE), f32(*MESSAGE), f32(*MESSAGE)]


def along_depth(value, by):
    count = lax.axis_size("depth")
    return lax.ppermute(value, "depth", [(i, i + by) for i in range(count) if 0 <= i + by < count])


def along_sky(value, by):
    count = lax.axis_size("sky")
    return lax.ppermute(value, "sky", [(i, (i + by) % count) for i in range(count)])


FORCE_SHAPE = (CELLS, 3 * BINS, 8, POINTS)
COUNT_SHAPE = (BINS, 8, POINTS)


def list_space(slots):
    return pltpu.SMEM((slots * BLOCKS + BLOCKS + 3 * UNROLL,), jnp.int32)


def stage_space():
    return [
        pltpu.VMEM((UNROLL, 3, STEP_ROWS, POINTS), jnp.float32),
        pltpu.VMEM((UNROLL, 5, STEP_ROWS, POINTS), jnp.float32),
    ]


def ghost_space(messages):
    slots = messages * SLOTS
    return (
        [pltpu.VMEM((slots * POINTS + STEP_ROWS, 8), jnp.float32)]
        + [list_space(slots)] * 4
        + [pltpu.SMEM((messages, 4, POINTS), jnp.float32), pltpu.SemaphoreType.DMA((messages,))]
        + stage_space()
    )


def cost(microseconds):
    return pl.CostEstimate(flops=0, transcendentals=0, bytes_accessed=int(microseconds * 3.0e6))


def self_pairs(target, cell_points):
    return pl.pallas_call(
        self_kernel,
        out_shape=[f32(*FORCE_SHAPE), f32(*COUNT_SHAPE)],
        in_specs=[VMEM, SMEM],
        out_specs=[VMEM] * 2,
        scratch_shapes=[pltpu.VMEM((CELLS * POINTS + STEP_ROWS, 8), jnp.float32)]
        + [list_space(CELLS)] * 2
        + stage_space(),
        compiler_params=PARAMS,
        cost_estimate=cost(6),
        name="self",
    )(target, cell_points)


def near_pairs(target, tables, from_below, from_above, force, counts):
    return pl.pallas_call(
        near_kernel,
        out_shape=[f32(*FORCE_SHAPE), f32(*COUNT_SHAPE)],
        in_specs=[VMEM] + [SMEM] * 4 + [VMEM] * 4,
        out_specs=[VMEM] * 2,
        scratch_shapes=ghost_space(2),
        input_output_aliases={7: 0, 8: 1},
        compiler_params=PARAMS,
        cost_estimate=cost(4),
        name="near",
    )(target, *tables[1:], from_below, from_above, force, counts)


def far_pairs(target, tables, from_left, from_right, force, counts):
    return pl.pallas_call(
        far_kernel,
        out_shape=[f32(*FORCE_SHAPE), f32(*COUNT_SHAPE), f32(*GRAD_SHAPE), f32(tables[1].shape[1], 2, POINTS)],
        in_specs=[VMEM] + [SMEM] * 5 + [VMEM] * 4,
        out_specs=[VMEM] * 4,
        scratch_shapes=ghost_space(6),
        input_output_aliases={8: 0, 9: 1},
        compiler_params=PARAMS,
        cost_estimate=cost(12),
        name="far",
    )(target, *tables, from_left, from_right, force, counts)[2:]


def body(positions, cell_points, target_log, export_count, export_cell, import_pair, import_shift):
    devices = export_count.shape[1]
    tables = (
        cell_points,
        export_count,
        jnp.transpose(export_cell[0], (1, 0)),
        jnp.transpose(import_pair[0], (1, 0)),
        jnp.transpose(import_shift[:, 0], (0, 2, 1)).reshape(3 * SLOTS, devices),
    )
    target, *messages = pl.pallas_call(
        first_kernel,
        out_shape=[f32(*CELL_SHAPE)] + MESSAGES,
        in_specs=[VMEM] + [SMEM] * 5,
        out_specs=[VMEM] * 5,
        scratch_shapes=[pltpu.VMEM(CELL_SHAPE, jnp.float32)],
        compiler_params=PARAMS,
        name="first",
    )(positions, *tables)
    for iteration in range(STEPS):
        depth_up, depth_down, sky_up, sky_down = messages
        from_below = along_depth(depth_up, 1)
        from_above = along_depth(depth_down, -1)
        from_below, from_above, force, counts = lax.optimization_barrier(
            (from_below, from_above, *self_pairs(target, cell_points))
        )
        near = near_pairs(target, tables, from_below, from_above, force, counts)
        from_left = along_sky(jnp.stack([sky_up, from_below[2], from_above[2]]), 1)
        from_right = along_sky(jnp.stack([sky_down, from_below[0], from_above[0]]), -1)
        grad, payload = far_pairs(target, tables, from_left, from_right, *near)
        sums = lax.all_to_all(payload, AXES, 0, 0)
        if iteration == STEPS - 1:
            return pl.pallas_call(
                last_kernel,
                out_shape=f32(*positions.shape),
                in_specs=[VMEM] * 3 + [SMEM],
                out_specs=VMEM,
                compiler_params=PARAMS,
                name="last",
            )(sums, grad, travel, target_log)
        travel, target, *messages = pl.pallas_call(
            update_kernel,
            out_shape=[f32(*CELL_SHAPE), f32(*CELL_SHAPE)] + MESSAGES,
            in_specs=[VMEM] * 3 + [SMEM] * 6,
            out_specs=[VMEM] * 6,
            scratch_shapes=[pltpu.VMEM(CELL_SHAPE, jnp.float32)],
            compiler_params=PARAMS,
            name="update",
        )(sums, grad, target, target_log, *tables)


def solution(mesh):
    in_specs = (
        P(None, ("sky", "depth"), None),
        P(("sky", "depth")),
        P(),
        P(("sky", "depth"), None),
        P(("sky", "depth"), None, None),
        P(("sky", "depth"), None, None),
        P(None, ("sky", "depth"), None, None),
    )
    out_specs = P(None, ("sky", "depth"), None)
    return jax.shard_map(body, mesh=mesh, in_specs=in_specs, out_specs=out_specs, check_vma=False)
```

```python
import functools
import math

import jax
import jax.numpy as jnp
from jax import lax
from jax.experimental import pallas as pl
from jax.experimental.pallas import tpu as pltpu
from jax.sharding import PartitionSpec as P

STEPS = 2
EPS_SQ = 0.0001
STEP_SIZE = 0.01

BINS = 16
CELLS = 16
POINTS = 128
SLOTS = 3
AXES = ("sky", "depth")

UNIT = math.sqrt(128.0 * math.log2(math.e))
CENTRES = [(b + 0.5) / 16.0 for b in range(BINS)]
CHAIN = 4
LIFT = 64.0
MIDDLE = CENTRES[8]
RADIUS_CAP = 2.1 * UNIT
FAR = 1.0e4
COUNT_SCALE = [
    math.exp(16.0 * (b % CHAIN) * (MIDDLE - CENTRES[b - b % CHAIN]) - 0.5 * (b % CHAIN) ** 2) * 2.0**-LIFT
    for b in range(BINS)
]
FORCE_SCALE = [-256.0 / UNIT * scale for scale in COUNT_SCALE]

NEIGHBOURS = [(0, 1), (0, 2), (1, 0), (1, 1), (1, 2), (2, 0), (2, 1), (2, 2)]
TABLE_ROW = 16
EXPORT, IMPORT, LIVE, SHIFT = 0, SLOTS, 2 * SLOTS, 2 * SLOTS + 1
SIZES = len(NEIGHBOURS) * TABLE_ROW
TABLE = SIZES + CELLS
STEP_ROWS = 16
BLOCKS = POINTS // STEP_ROWS
UNROLL = 2

VMEM = pl.BlockSpec(memory_space=pltpu.VMEM)
SMEM = pl.BlockSpec(memory_space=pltpu.SMEM)
PARAMS = pltpu.CompilerParams(vmem_limit_bytes=40 * 1024 * 1024)


def partner(axis, option):
    here = lax.axis_index(axis)
    if option == 0:
        return here
    step = 1 - 2 * (here % 2)
    return here + step if option == 1 else here - step


def neighbour(sky_option, depth_option):
    sky_count, depth_count = lax.axis_size("sky"), lax.axis_size("depth")
    sky = lax.rem(partner("sky", sky_option) + sky_count, sky_count)
    depth = partner("depth", depth_option)
    inside = (depth >= 0) & (depth < depth_count)
    return sky * depth_count + jnp.clip(depth, 0, depth_count - 1), inside


def column(values, shape):
    rows = lax.broadcasted_iota(jnp.int32, shape, 0)
    out = jnp.full(shape, values[0], jnp.float32)
    for index in range(1, len(values)):
        out = jnp.where(rows == index, values[index], out)
    return out


def shift_of(table, index, slot):
    rows = lax.broadcasted_iota(jnp.int32, (4, POINTS), 0)
    shift = jnp.zeros((4, POINTS), jnp.float32)
    for axis in range(3):
        amount = table[index * TABLE_ROW + SHIFT + axis * SLOTS + slot].astype(jnp.float32) * UNIT
        shift = jnp.where(rows == axis, amount, shift)
    return shift


def pack(source, table, outs):
    depth_even, depth_odd, sky_even, sky_odd = outs
    lanes = lax.broadcasted_iota(jnp.int32, (4, POINTS), 1)
    for index, (sky_option, depth_option) in enumerate(NEIGHBOURS):
        if depth_option == 0:
            out = sky_even if sky_option == 1 else sky_odd
        else:
            out = (depth_even if depth_option == 1 else depth_odd).at[sky_option]
        row = index * TABLE_ROW
        live = table[row + LIVE]
        meta = jnp.zeros((4, POINTS), jnp.float32)
        for slot in range(SLOTS):
            right = table[row + EXPORT + slot]
            out[slot] = source[right]
            size = jnp.where(slot < live, table[SIZES + right], 0)
            meta = jnp.where(lanes == slot, size.astype(jnp.float32), meta)
            left = table[row + IMPORT + slot]
            out[SLOTS + slot] = source[left] - shift_of(table, index, slot)
            size = table[SIZES + left]
            meta = jnp.where(lanes == SLOTS + slot, size.astype(jnp.float32), meta)
        out[2 * SLOTS] = meta


def first_kernel(
    positions_in, points_in, logs_in, count_in, export_in, import_in, shift_in,
    target, logs, table, depth_even, depth_odd, sky_even, sky_odd,
    positions, points, log_list, count, exports, imports, shifts, source, sems,
):
    pairs = [
        (points_in, points), (count_in, count), (export_in, exports), (import_in, imports),
        (shift_in, shifts), (positions_in, positions), (logs_in, log_list),
    ]
    copies = [
        pltpu.make_async_copy(origin, place, sems.at[index])
        for index, (origin, place) in enumerate(pairs)
    ]
    for copy in copies:
        copy.start()
    for copy in copies:
        copy.wait()
    for cell in range(CELLS):
        table[SIZES + cell] = points[cell]
    for index, options in enumerate(NEIGHBOURS):
        device, inside = neighbour(*options)
        row = index * TABLE_ROW
        table[row + LIVE] = jnp.where(inside, count[0, device], 0)
        for slot in range(SLOTS):
            table[row + EXPORT + slot] = exports[slot, 0, device]
            table[row + IMPORT + slot] = imports[slot, 0, device]
            for axis in range(3):
                table[row + SHIFT + axis * SLOTS + slot] = shifts[axis, slot, 0, device]
    logs[...] = column([log_list[b] for b in range(BINS)], (BINS, POINTS))
    lanes = lax.broadcasted_iota(jnp.int32, (4, POINTS), 1)
    for cell in range(CELLS):
        rows = [positions[axis, cell : cell + 1, :] for axis in range(3)]
        tile = jnp.concatenate(rows + [jnp.zeros((1, POINTS), jnp.float32)], axis=0) * UNIT
        live = lanes < points[cell]
        target[cell] = jnp.where(live, tile, -FAR)
        source[cell] = jnp.where(live, tile, FAR)
    pack(source, table, (depth_even, depth_odd, sky_even, sky_odd))


def spread_points(at, row_list, source, base, spread):
    blocks = [
        source[pl.ds(pl.multiple_of(row_list[at + unit] * STEP_ROWS, STEP_ROWS), STEP_ROWS), :]
        for unit in range(UNROLL)
    ]
    for axis in range(3):
        for unit in range(UNROLL):
            lane = base + axis
            spread[unit, axis] = jnp.broadcast_to(blocks[unit][:, lane : lane + 1], (STEP_ROWS, POINTS))


def shape_pairs(at, cell_list, target, spread, shapes):
    for unit in range(UNROLL):
        cell = cell_list[at + unit]
        dx, dy, dz = (target[cell, axis : axis + 1, :] - spread[unit, axis] for axis in range(3))
        square = dx * dx + dy * dy + dz * dz + EPS_SQ * UNIT * UNIT
        inverse = lax.rsqrt(square)
        radius = jnp.minimum(square * inverse, RADIUS_CAP)
        ratio = jnp.exp2(
            radius * (16.0 * math.log2(math.e) / UNIT) - 16.0 * math.log2(math.e) * MIDDLE
        )
        for index, value in enumerate((radius, ratio, dx * inverse, dy * inverse, dz * inverse)):
            shapes[unit, index] = value


def add_block(values, cell, force, counts):
    radius, ratio, *units = values
    for chain in range(BINS // CHAIN):
        for link in range(CHAIN):
            b = chain * CHAIN + link
            delta = radius - CENTRES[b] * UNIT
            if link == 0:
                value = jnp.exp2(LIFT - delta * delta)
            else:
                value = value * ratio
            if counts is not None:
                counts[b] += value[:8] + value[8:]
            slope = value * delta
            for axis in range(3):
                pulled = slope * units[axis]
                force[cell, axis * BINS + b] += pulled[:8] + pulled[8:]


def add_blocks(total, row_list, cell_list, base, target, source, force, counts, spread, shapes):
    spread_points(0, row_list, source, base, spread)
    shape_pairs(0, cell_list, target, spread, shapes)
    spread_points(UNROLL, row_list, source, base, spread)

    def step(turn, unused):
        at = turn * UNROLL
        now = [[shapes[unit, index] for index in range(5)] for unit in range(UNROLL)]
        shape_pairs(at + UNROLL, cell_list, target, spread, shapes)
        spread_points(at + 2 * UNROLL, row_list, source, base, spread)
        for unit in range(UNROLL):
            add_block(now[unit], cell_list[at + unit], force, counts)
        return unused

    lax.fori_loop(0, (total + (UNROLL - 1)) // UNROLL, step, 0)


def list_blocks(at, slot, cell, size, row_list, cell_list):
    for block in range(BLOCKS):
        row_list[at + block] = slot * BLOCKS + block
        cell_list[at + block] = cell
    return at + (size + (STEP_ROWS - 1)) // STEP_ROWS


def end_list(at, slots, row_list, cell_list):
    for spare in range(3 * UNROLL):
        row_list[at + spare] = slots * BLOCKS
        cell_list[at + spare] = 0


def put_points(source, slot, first, second):
    source[slot * POINTS : (slot + 1) * POINTS] = jnp.transpose(
        jnp.concatenate([first, second], axis=0), (1, 0)
    )


def self_kernel(target, table, force, counts, source, row_list, cell_list, spread, shapes):
    lanes = lax.broadcasted_iota(jnp.int32, (4, POINTS), 1)
    end = 0
    for cell in range(CELLS):
        size = table[SIZES + cell]
        tile = jnp.where(lanes < size, target[cell], FAR)
        put_points(source, cell, tile, tile)
        end = list_blocks(end, cell, cell, size, row_list, cell_list)
    end_list(end, CELLS, row_list, cell_list)
    source[CELLS * POINTS :] = jnp.full((STEP_ROWS, 8), FAR, jnp.float32)
    force[...] = jnp.zeros(force.shape, jnp.float32)
    counts[...] = jnp.zeros(counts.shape, jnp.float32)
    add_blocks(end, row_list, cell_list, 0, target, source, force, counts, spread, shapes)
    counts[...] = 0.5 * counts[...]


def ghost_pairs(
    messages, metas, first, target, table, force, counts,
    source, import_rows, import_cells, export_rows, export_cells, meta, sems, spread, shapes,
):
    copies = []
    at = 0
    for index, part in enumerate(metas):
        size = part.shape[0]
        copies.append(pltpu.make_async_copy(part, meta.at[at : at + size], sems.at[index]))
        at += size
    for copy in copies:
        copy.start()
    for index, message in enumerate(messages):
        for slot in range(SLOTS):
            put_points(
                source, index * SLOTS + slot,
                message[slot] + shift_of(table, first + index, slot), message[SLOTS + slot],
            )
    slots = len(messages) * SLOTS
    source[slots * POINTS :] = jnp.full((STEP_ROWS, 8), FAR, jnp.float32)
    for copy in copies:
        copy.wait()
    import_end = 0
    export_end = 0
    for index in range(len(messages)):
        row = (first + index) * TABLE_ROW
        live = table[row + LIVE]
        for slot in range(SLOTS):
            at = index * SLOTS + slot
            size = meta[index, 0, slot].astype(jnp.int32)
            import_end = list_blocks(
                import_end, at, table[row + IMPORT + slot], size, import_rows, import_cells
            )
            size = jnp.where(slot < live, meta[index, 0, SLOTS + slot].astype(jnp.int32), 0)
            export_end = list_blocks(
                export_end, at, table[row + EXPORT + slot], size, export_rows, export_cells
            )
    end_list(import_end, slots, import_rows, import_cells)
    end_list(export_end, slots, export_rows, export_cells)
    add_blocks(
        import_end, import_rows, import_cells, 0, target, source, force, counts, spread, shapes
    )
    add_blocks(
        export_end, export_rows, export_cells, 4, target, source, force, None, spread, shapes
    )


def near_kernel(target, table, from_even, from_odd, force_in, counts_in, force, counts, *scratch):
    ghost_pairs(
        [from_even.at[0], from_odd.at[0]],
        [side.at[0:1, 2 * SLOTS] for side in (from_even, from_odd)],
        0, target, table, force, counts, *scratch,
    )


def far_kernel(
    target, table, from_even, from_odd, force_in, counts_in, force, counts, grad, payload, *scratch,
):
    ghost_pairs(
        [side.at[index] for side in (from_even, from_odd) for index in range(3)],
        [side.at[:, 2 * SLOTS] for side in (from_even, from_odd)],
        2, target, table, force, counts, *scratch,
    )
    force_scale = column(FORCE_SCALE, (BINS, POINTS))
    for cell in range(CELLS):
        for axis in range(3):
            tile = jnp.sum(force[cell, axis * BINS : (axis + 1) * BINS], axis=1) * force_scale
            at = (cell * 3 + axis) * POINTS
            grad[:, at : at + POINTS] = tile
    whole = grad[...]
    gram = lax.dot_general(
        whole, whole, (((1,), (1,)), ((), ())),
        precision=lax.Precision.HIGHEST, preferred_element_type=jnp.float32,
    )
    bins = lax.broadcasted_iota(jnp.int32, (BINS, POINTS), 0)
    lane = lax.broadcasted_iota(jnp.int32, (BINS, POINTS), 1)
    low, high = lane % BINS, lane // BINS
    spread = jnp.where(low == bins, 1.0, 0.0)
    wide = lax.dot_general(
        gram, spread, (((1,), (0,)), ((), ())),
        precision=lax.Precision.HIGHEST, preferred_element_type=jnp.float32,
    )
    first = jnp.sum(jnp.where(bins == (low + high) % BINS, wide, 0.0), axis=0, keepdims=True)
    second = jnp.where((bins == (low + 8) % BINS) & (high == 0), wide, 0.0)
    sums = jnp.sum(counts[...], axis=1)
    sums = jnp.sum(sums, axis=1, keepdims=True) * column(COUNT_SCALE, (BINS, POINTS))
    second = second + jnp.where(lane == bins + BINS, sums, 0.0)
    total = table[SIZES]
    for cell in range(1, CELLS):
        total = total + table[SIZES + cell]
    second = second + jnp.where((lane == 2 * BINS) & (bins == 0), total.astype(jnp.float32), 0.0)
    second = jnp.sum(second, axis=0, keepdims=True)
    both = jnp.concatenate([first, second], axis=0)
    payload[...] = jnp.broadcast_to(both[None], payload.shape)


def moves_of(sums, grad, logs):
    both = jnp.sum(sums[...], axis=0)
    bins = lax.broadcasted_iota(jnp.int32, (BINS, POINTS), 0)
    lane = lax.broadcasted_iota(jnp.int32, (BINS, POINTS), 1)
    low, high = lane % BINS, lane // BINS
    first, second = both[0:1], both[1:2]
    counts = jnp.sum(
        jnp.where(lane == bins + BINS, jnp.broadcast_to(second, (BINS, POINTS)), 0.0), axis=1, keepdims=True
    )
    counts = jnp.broadcast_to(counts, (BINS, POINTS))
    one_lane = lax.broadcasted_iota(jnp.int32, (1, POINTS), 1)
    valid = jnp.sum(jnp.where(one_lane == 2 * BINS, second, 0.0), axis=1, keepdims=True)
    mean_count = jnp.sum(counts, axis=0, keepdims=True) / BINS
    pull = (jnp.log(1.0 + counts) - logs[...]) * mean_count / (1.0 + counts)
    here = jnp.sum(jnp.where(bins == low, pull, 0.0), axis=0, keepdims=True)
    there = jnp.sum(jnp.where(bins == (low + high) % BINS, pull, 0.0), axis=0, keepdims=True)
    across = jnp.sum(jnp.where(bins == (low + 8) % BINS, pull, 0.0), axis=0, keepdims=True)
    power = first * here * there * jnp.where(one_lane < BINS, 1.0, 2.0)
    power = power + jnp.where(one_lane < BINS, second * here * across, 0.0)
    power = jnp.maximum(jnp.sum(power, axis=1, keepdims=True), 0.0)
    rms = jnp.sqrt(power / (3.0 * valid) + 1e-06)
    weights = pull / -rms
    out = []
    for cell in range(CELLS):
        parts = []
        for axis in range(3):
            at = (cell * 3 + axis) * POINTS
            parts.append(jnp.sum(grad[:, at : at + POINTS] * weights, axis=0, keepdims=True))
        out.append(parts)
    return out


def update_kernel(
    sums, grad, target, logs, table,
    travel, next_target, depth_even, depth_odd, sky_even, sky_odd, source,
):
    lanes = lax.broadcasted_iota(jnp.int32, (4, POINTS), 1)
    moves = moves_of(sums, grad, logs)
    for cell in range(CELLS):
        tile = jnp.concatenate(moves[cell] + [jnp.zeros((1, POINTS), jnp.float32)], axis=0)
        travel[cell] = tile
        tile = target[cell] + (STEP_SIZE * UNIT) * tile
        next_target[cell] = tile
        source[cell] = jnp.where(lanes < table[SIZES + cell], tile, FAR)
    pack(source, table, (depth_even, depth_odd, sky_even, sky_odd))


def last_kernel(sums, grad, travel, logs, out):
    moves = moves_of(sums, grad, logs)
    for cell in range(CELLS):
        for axis in range(3):
            out[axis, cell : cell + 1, :] = travel[cell, axis : axis + 1, :] + moves[cell][axis]


def f32(*shape):
    return jax.ShapeDtypeStruct(shape, jnp.float32)


CELL_SHAPE = (CELLS, 4, POINTS)
GRAD_SHAPE = (BINS, CELLS * 3 * POINTS)
MESSAGE = (2 * SLOTS + 1, 4, POINTS)
MESSAGES = [f32(3, *MESSAGE), f32(3, *MESSAGE), f32(*MESSAGE), f32(*MESSAGE)]


def swap(value, axis, option):
    count = lax.axis_size(axis)
    perm = []
    for low in range(option - 1, count, 2):
        high = low + 1
        if high < count or axis == "sky":
            perm += [(low, high % count), (high % count, low)]
    return lax.ppermute(value, axis, perm)


FORCE_SHAPE = (CELLS, 3 * BINS, 8, POINTS)
COUNT_SHAPE = (BINS, 8, POINTS)


def list_space(slots):
    return pltpu.SMEM((slots * BLOCKS + BLOCKS + 3 * UNROLL,), jnp.int32)


def stage_space():
    return [
        pltpu.VMEM((UNROLL, 3, STEP_ROWS, POINTS), jnp.float32),
        pltpu.VMEM((UNROLL, 5, STEP_ROWS, POINTS), jnp.float32),
    ]


def ghost_space(messages):
    slots = messages * SLOTS
    return (
        [pltpu.VMEM((slots * POINTS + STEP_ROWS, 8), jnp.float32)]
        + [list_space(slots)] * 4
        + [pltpu.SMEM((messages, 4, POINTS), jnp.float32), pltpu.SemaphoreType.DMA((2,))]
        + stage_space()
    )


def cost(microseconds):
    return pl.CostEstimate(flops=0, transcendentals=0, bytes_accessed=int(microseconds * 3.0e6))


def self_pairs(target, table):
    return pl.pallas_call(
        self_kernel,
        out_shape=[f32(*FORCE_SHAPE), f32(*COUNT_SHAPE)],
        in_specs=[VMEM, SMEM],
        out_specs=[VMEM] * 2,
        scratch_shapes=[pltpu.VMEM((CELLS * POINTS + STEP_ROWS, 8), jnp.float32)]
        + [list_space(CELLS)] * 2
        + stage_space(),
        compiler_params=PARAMS,
        cost_estimate=cost(6),
        name="self",
    )(target, table)


def near_pairs(target, table, from_even, from_odd, force, counts):
    return pl.pallas_call(
        near_kernel,
        out_shape=[f32(*FORCE_SHAPE), f32(*COUNT_SHAPE)],
        in_specs=[VMEM, SMEM] + [VMEM] * 4,
        out_specs=[VMEM] * 2,
        scratch_shapes=ghost_space(2),
        input_output_aliases={4: 0, 5: 1},
        compiler_params=PARAMS,
        cost_estimate=cost(4),
        name="near",
    )(target, table, from_even, from_odd, force, counts)


def far_pairs(devices, target, table, from_even, from_odd, force, counts):
    return pl.pallas_call(
        far_kernel,
        out_shape=[f32(*FORCE_SHAPE), f32(*COUNT_SHAPE), f32(*GRAD_SHAPE), f32(devices, 2, POINTS)],
        in_specs=[VMEM, SMEM] + [VMEM] * 4,
        out_specs=[VMEM] * 4,
        scratch_shapes=ghost_space(6),
        input_output_aliases={4: 0, 5: 1},
        compiler_params=PARAMS,
        cost_estimate=cost(12),
        name="far",
    )(target, table, from_even, from_odd, force, counts)[2:]


def body(positions, cell_points, target_log, export_count, export_cell, import_pair, import_shift):
    devices = export_count.shape[1]
    inputs = (
        positions, cell_points, target_log, export_count,
        jnp.transpose(export_cell, (2, 0, 1)),
        jnp.transpose(import_pair, (2, 0, 1)),
        jnp.transpose(import_shift, (0, 3, 1, 2)),
    )
    target, logs, table, *messages = pl.pallas_call(
        first_kernel,
        out_shape=[f32(*CELL_SHAPE), f32(BINS, POINTS), jax.ShapeDtypeStruct((TABLE,), jnp.int32)] + MESSAGES,
        in_specs=[pl.BlockSpec(memory_space=pltpu.HBM)] * 7,
        out_specs=[VMEM, VMEM, SMEM] + [VMEM] * 4,
        scratch_shapes=[
            pltpu.VMEM(positions.shape, jnp.float32),
            pltpu.SMEM(cell_points.shape, jnp.int32),
            pltpu.SMEM(target_log.shape, jnp.float32),
            pltpu.SMEM(export_count.shape, jnp.int32),
            pltpu.SMEM((SLOTS, 1, devices), jnp.int32),
            pltpu.SMEM((SLOTS, 1, devices), jnp.int32),
            pltpu.SMEM((3, SLOTS, 1, devices), jnp.int32),
            pltpu.VMEM(CELL_SHAPE, jnp.float32),
            pltpu.SemaphoreType.DMA((7,)),
        ],
        compiler_params=PARAMS,
        name="first",
    )(*(pltpu.with_memory_space_constraint(value, pltpu.HBM) for value in inputs))
    for iteration in range(STEPS):
        depth_even, depth_odd, sky_even, sky_odd = messages
        depth_even, depth_odd = swap(depth_even, "depth", 1), swap(depth_odd, "depth", 2)
        depth_even, depth_odd, force, counts = lax.optimization_barrier(
            (depth_even, depth_odd, *self_pairs(target, table))
        )
        near = near_pairs(target, table, depth_even, depth_odd, force, counts)
        sky_even = swap(jnp.stack([sky_even, depth_even[1], depth_odd[1]]), "sky", 1)
        sky_odd = swap(jnp.stack([sky_odd, depth_even[2], depth_odd[2]]), "sky", 2)
        grad, payload = far_pairs(devices, target, table, sky_even, sky_odd, *near)
        sums = lax.all_to_all(payload, AXES, 0, 0)
        if iteration == STEPS - 1:
            return pl.pallas_call(
                last_kernel,
                out_shape=f32(*positions.shape),
                in_specs=[VMEM] * 4,
                out_specs=VMEM,
                compiler_params=PARAMS,
                name="last",
            )(sums, grad, travel, logs)
        travel, target, *messages = pl.pallas_call(
            update_kernel,
            out_shape=[f32(*CELL_SHAPE), f32(*CELL_SHAPE)] + MESSAGES,
            in_specs=[VMEM] * 4 + [SMEM],
            out_specs=[VMEM] * 6,
            scratch_shapes=[pltpu.VMEM(CELL_SHAPE, jnp.float32)],
            compiler_params=PARAMS,
            name="update",
        )(sums, grad, target, logs, table)


def solution(mesh):
    in_specs = (
        P(None, ("sky", "depth"), None),
        P(("sky", "depth")),
        P(),
        P(("sky", "depth"), None),
        P(("sky", "depth"), None, None),
        P(("sky", "depth"), None, None),
        P(None, ("sky", "depth"), None, None),
    )
    out_specs = P(None, ("sky", "depth"), None)
    return jax.shard_map(body, mesh=mesh, in_specs=in_specs, out_specs=out_specs, check_vma=False)
```

```python
import functools
import math

import jax
import jax.numpy as jnp
from jax import lax
from jax.experimental import pallas as pl
from jax.experimental.pallas import tpu as pltpu
from jax.sharding import PartitionSpec as P

STEPS = 2
EPS_SQ = 0.0001
STEP_SIZE = 0.01

BINS = 16
CELLS = 16
POINTS = 128
SLOTS = 3
AXES = ("sky", "depth")

UNIT = math.sqrt(128.0 * math.log2(math.e))
CENTRES = [(b + 0.5) / 16.0 for b in range(BINS)]
CHAIN = 4
LIFT = 64.0
MIDDLE = CENTRES[8]
RADIUS_CAP = 2.1 * UNIT
FAR = 1.0e4
COUNT_SCALE = [
    math.exp(16.0 * (b % CHAIN) * (MIDDLE - CENTRES[b - b % CHAIN]) - 0.5 * (b % CHAIN) ** 2) * 2.0**-LIFT
    for b in range(BINS)
]
FORCE_SCALE = [-256.0 / UNIT * scale for scale in COUNT_SCALE]

NEIGHBOURS = [(0, 1), (0, 2), (1, 0), (1, 1), (1, 2), (2, 0), (2, 1), (2, 2)]
TABLE_ROW = 16
EXPORT, IMPORT, LIVE, SHIFT = 0, SLOTS, 2 * SLOTS, 2 * SLOTS + 1
SIZES = len(NEIGHBOURS) * TABLE_ROW
TABLE = SIZES + CELLS
STEP_ROWS = 16
BLOCKS = POINTS // STEP_ROWS
UNROLL = 4

VMEM = pl.BlockSpec(memory_space=pltpu.VMEM)
SMEM = pl.BlockSpec(memory_space=pltpu.SMEM)
PARAMS = pltpu.CompilerParams(vmem_limit_bytes=40 * 1024 * 1024)


def partner(axis, option):
    here = lax.axis_index(axis)
    if option == 0:
        return here
    step = 1 - 2 * (here % 2)
    return here + step if option == 1 else here - step


def neighbour(sky_option, depth_option):
    sky_count, depth_count = lax.axis_size("sky"), lax.axis_size("depth")
    sky = lax.rem(partner("sky", sky_option) + sky_count, sky_count)
    depth = partner("depth", depth_option)
    inside = (depth >= 0) & (depth < depth_count)
    return sky * depth_count + jnp.clip(depth, 0, depth_count - 1), inside


def column(values, shape):
    rows = lax.broadcasted_iota(jnp.int32, shape, 0)
    out = jnp.full(shape, values[0], jnp.float32)
    for index in range(1, len(values)):
        out = jnp.where(rows == index, values[index], out)
    return out


def shift_of(table, index, slot):
    rows = lax.broadcasted_iota(jnp.int32, (4, POINTS), 0)
    shift = jnp.zeros((4, POINTS), jnp.float32)
    for axis in range(3):
        amount = table[index * TABLE_ROW + SHIFT + axis * SLOTS + slot].astype(jnp.float32) * UNIT
        shift = jnp.where(rows == axis, amount, shift)
    return shift


def pack(source, table, outs):
    depth_even, depth_odd, sky_even, sky_odd = outs
    lanes = lax.broadcasted_iota(jnp.int32, (4, POINTS), 1)
    for index, (sky_option, depth_option) in enumerate(NEIGHBOURS):
        if depth_option == 0:
            out = sky_even if sky_option == 1 else sky_odd
        else:
            out = (depth_even if depth_option == 1 else depth_odd).at[sky_option]
        row = index * TABLE_ROW
        live = table[row + LIVE]
        meta = jnp.zeros((4, POINTS), jnp.float32)
        for slot in range(SLOTS):
            right = table[row + EXPORT + slot]
            out[slot] = source[right]
            size = jnp.where(slot < live, table[SIZES + right], 0)
            meta = jnp.where(lanes == slot, size.astype(jnp.float32), meta)
            left = table[row + IMPORT + slot]
            out[SLOTS + slot] = source[left] - shift_of(table, index, slot)
            size = table[SIZES + left]
            meta = jnp.where(lanes == SLOTS + slot, size.astype(jnp.float32), meta)
        out[2 * SLOTS] = meta


def first_kernel(
    positions_in, points_in, logs_in, count_in, export_in, import_in, shift_in,
    target, logs, table, depth_even, depth_odd, sky_even, sky_odd,
    positions, points, log_list, count, exports, imports, shifts, source, sems,
):
    pairs = [
        (points_in, points), (count_in, count), (export_in, exports), (import_in, imports),
        (shift_in, shifts), (positions_in, positions), (logs_in, log_list),
    ]
    copies = [
        pltpu.make_async_copy(origin, place, sems.at[index])
        for index, (origin, place) in enumerate(pairs)
    ]
    for copy in copies:
        copy.start()
    for copy in copies:
        copy.wait()
    for cell in range(CELLS):
        table[SIZES + cell] = points[cell]
    for index, options in enumerate(NEIGHBOURS):
        device, inside = neighbour(*options)
        row = index * TABLE_ROW
        table[row + LIVE] = jnp.where(inside, count[0, device], 0)
        for slot in range(SLOTS):
            table[row + EXPORT + slot] = exports[slot, 0, device]
            table[row + IMPORT + slot] = imports[slot, 0, device]
            for axis in range(3):
                table[row + SHIFT + axis * SLOTS + slot] = shifts[axis, slot, 0, device]
    logs[...] = column([log_list[b] for b in range(BINS)], (BINS, POINTS))
    lanes = lax.broadcasted_iota(jnp.int32, (4, POINTS), 1)
    for cell in range(CELLS):
        rows = [positions[axis, cell : cell + 1, :] for axis in range(3)]
        tile = jnp.concatenate(rows + [jnp.zeros((1, POINTS), jnp.float32)], axis=0) * UNIT
        live = lanes < points[cell]
        target[cell] = jnp.where(live, tile, -FAR)
        source[cell] = jnp.where(live, tile, FAR)
    pack(source, table, (depth_even, depth_odd, sky_even, sky_odd))


def shape_pairs(at, row_list, cell_list, source, base, target):
    units = range(UNROLL)
    blocks = [
        source[pl.ds(pl.multiple_of(row_list[at + unit] * STEP_ROWS, STEP_ROWS), STEP_ROWS), :]
        for unit in units
    ]
    spread = [
        [
            jnp.broadcast_to(blocks[unit][:, base + axis : base + axis + 1], (STEP_ROWS, POINTS))
            for unit in units
        ]
        for axis in range(3)
    ]
    out = []
    for unit in units:
        cell = cell_list[at + unit]
        dx, dy, dz = (target[cell, axis : axis + 1, :] - spread[axis][unit] for axis in range(3))
        square = dx * dx + dy * dy + dz * dz + EPS_SQ * UNIT * UNIT
        inverse = lax.rsqrt(square)
        radius = jnp.minimum(square * inverse, RADIUS_CAP)
        ratio = jnp.exp2(
            radius * (16.0 * math.log2(math.e) / UNIT) - 16.0 * math.log2(math.e) * MIDDLE
        )
        out.append((radius, ratio, dx * inverse, dy * inverse, dz * inverse))
    return out


def add_block(values, cell, force, counts):
    radius, ratio, *units = values
    for chain in range(BINS // CHAIN):
        for link in range(CHAIN):
            b = chain * CHAIN + link
            delta = radius - CENTRES[b] * UNIT
            if link == 0:
                value = jnp.exp2(LIFT - delta * delta)
            else:
                value = value * ratio
            if counts is not None:
                counts[b] += value[:8] + value[8:]
            slope = value * delta
            for axis in range(3):
                pulled = slope * units[axis]
                force[cell, axis * BINS + b] += pulled[:8] + pulled[8:]


def add_blocks(total, row_list, cell_list, base, target, source, force, counts):
    def step(turn, shapes):
        at = turn * UNROLL
        ahead = shape_pairs(at + UNROLL, row_list, cell_list, source, base, target)
        for unit in range(UNROLL):
            add_block(shapes[unit], cell_list[at + unit], force, counts)
        return ahead

    first = shape_pairs(0, row_list, cell_list, source, base, target)
    lax.fori_loop(0, (total + (UNROLL - 1)) // UNROLL, step, first)


def list_blocks(at, slot, cell, size, row_list, cell_list):
    for block in range(BLOCKS):
        row_list[at + block] = slot * BLOCKS + block
        cell_list[at + block] = cell
    return at + (size + (STEP_ROWS - 1)) // STEP_ROWS


def end_list(at, slots, row_list, cell_list):
    for spare in range(3 * UNROLL):
        row_list[at + spare] = slots * BLOCKS
        cell_list[at + spare] = 0


def put_points(source, slot, first, second):
    source[slot * POINTS : (slot + 1) * POINTS] = jnp.transpose(
        jnp.concatenate([first, second], axis=0), (1, 0)
    )


def self_kernel(target, table, force, counts, source, row_list, cell_list):
    lanes = lax.broadcasted_iota(jnp.int32, (4, POINTS), 1)
    end = 0
    for cell in range(CELLS):
        size = table[SIZES + cell]
        tile = jnp.where(lanes < size, target[cell], FAR)
        put_points(source, cell, tile, tile)
        end = list_blocks(end, cell, cell, size, row_list, cell_list)
    end_list(end, CELLS, row_list, cell_list)
    source[CELLS * POINTS :] = jnp.full((STEP_ROWS, 8), FAR, jnp.float32)
    force[...] = jnp.zeros(force.shape, jnp.float32)
    counts[...] = jnp.zeros(counts.shape, jnp.float32)
    add_blocks(end, row_list, cell_list, 0, target, source, force, counts)
    counts[...] = 0.5 * counts[...]


def ghost_pairs(
    messages, metas, first, target, table, force, counts,
    source, import_rows, import_cells, export_rows, export_cells, meta, sems,
):
    copies = []
    at = 0
    for index, part in enumerate(metas):
        size = part.shape[0]
        copies.append(pltpu.make_async_copy(part, meta.at[at : at + size], sems.at[index]))
        at += size
    for copy in copies:
        copy.start()
    for index, message in enumerate(messages):
        for slot in range(SLOTS):
            put_points(
                source, index * SLOTS + slot,
                message[slot] + shift_of(table, first + index, slot), message[SLOTS + slot],
            )
    slots = len(messages) * SLOTS
    source[slots * POINTS :] = jnp.full((STEP_ROWS, 8), FAR, jnp.float32)
    for copy in copies:
        copy.wait()
    import_end = 0
    export_end = 0
    for index in range(len(messages)):
        row = (first + index) * TABLE_ROW
        live = table[row + LIVE]
        for slot in range(SLOTS):
            at = index * SLOTS + slot
            size = meta[index, 0, slot].astype(jnp.int32)
            import_end = list_blocks(
                import_end, at, table[row + IMPORT + slot], size, import_rows, import_cells
            )
            size = jnp.where(slot < live, meta[index, 0, SLOTS + slot].astype(jnp.int32), 0)
            export_end = list_blocks(
                export_end, at, table[row + EXPORT + slot], size, export_rows, export_cells
            )
    end_list(import_end, slots, import_rows, import_cells)
    end_list(export_end, slots, export_rows, export_cells)
    add_blocks(
        import_end, import_rows, import_cells, 0, target, source, force, counts
    )
    add_blocks(
        export_end, export_rows, export_cells, 4, target, source, force, None
    )


def near_kernel(target, table, from_even, from_odd, force_in, counts_in, force, counts, *scratch):
    ghost_pairs(
        [from_even.at[0], from_odd.at[0]],
        [side.at[0:1, 2 * SLOTS] for side in (from_even, from_odd)],
        0, target, table, force, counts, *scratch,
    )


def far_kernel(
    target, table, from_even, from_odd, force_in, counts_in, force, counts, grad, payload, *scratch,
):
    ghost_pairs(
        [side.at[index] for side in (from_even, from_odd) for index in range(3)],
        [side.at[:, 2 * SLOTS] for side in (from_even, from_odd)],
        2, target, table, force, counts, *scratch,
    )
    force_scale = column(FORCE_SCALE, (BINS, POINTS))
    for cell in range(CELLS):
        for axis in range(3):
            tile = jnp.sum(force[cell, axis * BINS : (axis + 1) * BINS], axis=1) * force_scale
            at = (cell * 3 + axis) * POINTS
            grad[:, at : at + POINTS] = tile
    whole = grad[...]
    gram = lax.dot_general(
        whole, whole, (((1,), (1,)), ((), ())),
        precision=lax.Precision.HIGHEST, preferred_element_type=jnp.float32,
    )
    bins = lax.broadcasted_iota(jnp.int32, (BINS, POINTS), 0)
    lane = lax.broadcasted_iota(jnp.int32, (BINS, POINTS), 1)
    low, high = lane % BINS, lane // BINS
    spread = jnp.where(low == bins, 1.0, 0.0)
    wide = lax.dot_general(
        gram, spread, (((1,), (0,)), ((), ())),
        precision=lax.Precision.HIGHEST, preferred_element_type=jnp.float32,
    )
    first = jnp.sum(jnp.where(bins == (low + high) % BINS, wide, 0.0), axis=0, keepdims=True)
    second = jnp.where((bins == (low + 8) % BINS) & (high == 0), wide, 0.0)
    sums = jnp.sum(counts[...], axis=1)
    sums = jnp.sum(sums, axis=1, keepdims=True) * column(COUNT_SCALE, (BINS, POINTS))
    second = second + jnp.where(lane == bins + BINS, sums, 0.0)
    total = table[SIZES]
    for cell in range(1, CELLS):
        total = total + table[SIZES + cell]
    second = second + jnp.where((lane == 2 * BINS) & (bins == 0), total.astype(jnp.float32), 0.0)
    second = jnp.sum(second, axis=0, keepdims=True)
    both = jnp.concatenate([first, second], axis=0)
    payload[...] = jnp.broadcast_to(both[None], payload.shape)


def moves_of(sums, grad, logs):
    both = jnp.sum(sums[...], axis=0)
    bins = lax.broadcasted_iota(jnp.int32, (BINS, POINTS), 0)
    lane = lax.broadcasted_iota(jnp.int32, (BINS, POINTS), 1)
    low, high = lane % BINS, lane // BINS
    first, second = both[0:1], both[1:2]
    counts = jnp.sum(
        jnp.where(lane == bins + BINS, jnp.broadcast_to(second, (BINS, POINTS)), 0.0), axis=1, keepdims=True
    )
    counts = jnp.broadcast_to(counts, (BINS, POINTS))
    one_lane = lax.broadcasted_iota(jnp.int32, (1, POINTS), 1)
    valid = jnp.sum(jnp.where(one_lane == 2 * BINS, second, 0.0), axis=1, keepdims=True)
    mean_count = jnp.sum(counts, axis=0, keepdims=True) / BINS
    pull = (jnp.log(1.0 + counts) - logs[...]) * mean_count / (1.0 + counts)
    here = jnp.sum(jnp.where(bins == low, pull, 0.0), axis=0, keepdims=True)
    there = jnp.sum(jnp.where(bins == (low + high) % BINS, pull, 0.0), axis=0, keepdims=True)
    across = jnp.sum(jnp.where(bins == (low + 8) % BINS, pull, 0.0), axis=0, keepdims=True)
    power = first * here * there * jnp.where(one_lane < BINS, 1.0, 2.0)
    power = power + jnp.where(one_lane < BINS, second * here * across, 0.0)
    power = jnp.maximum(jnp.sum(power, axis=1, keepdims=True), 0.0)
    rms = jnp.sqrt(power / (3.0 * valid) + 1e-06)
    weights = pull / -rms
    out = []
    for cell in range(CELLS):
        parts = []
        for axis in range(3):
            at = (cell * 3 + axis) * POINTS
            parts.append(jnp.sum(grad[:, at : at + POINTS] * weights, axis=0, keepdims=True))
        out.append(parts)
    return out


def update_kernel(
    sums, grad, target, logs, table,
    travel, next_target, depth_even, depth_odd, sky_even, sky_odd, source,
):
    lanes = lax.broadcasted_iota(jnp.int32, (4, POINTS), 1)
    moves = moves_of(sums, grad, logs)
    for cell in range(CELLS):
        tile = jnp.concatenate(moves[cell] + [jnp.zeros((1, POINTS), jnp.float32)], axis=0)
        travel[cell] = tile
        tile = target[cell] + (STEP_SIZE * UNIT) * tile
        next_target[cell] = tile
        source[cell] = jnp.where(lanes < table[SIZES + cell], tile, FAR)
    pack(source, table, (depth_even, depth_odd, sky_even, sky_odd))


def last_kernel(sums, grad, travel, logs, out):
    moves = moves_of(sums, grad, logs)
    for cell in range(CELLS):
        for axis in range(3):
            out[axis, cell : cell + 1, :] = travel[cell, axis : axis + 1, :] + moves[cell][axis]


def f32(*shape):
    return jax.ShapeDtypeStruct(shape, jnp.float32)


CELL_SHAPE = (CELLS, 4, POINTS)
GRAD_SHAPE = (BINS, CELLS * 3 * POINTS)
MESSAGE = (2 * SLOTS + 1, 4, POINTS)
MESSAGES = [f32(3, *MESSAGE), f32(3, *MESSAGE), f32(*MESSAGE), f32(*MESSAGE)]


def swap(value, axis, option):
    count = lax.axis_size(axis)
    perm = []
    for low in range(option - 1, count, 2):
        high = low + 1
        if high < count or axis == "sky":
            perm += [(low, high % count), (high % count, low)]
    return lax.ppermute(value, axis, perm)


FORCE_SHAPE = (CELLS, 3 * BINS, 8, POINTS)
COUNT_SHAPE = (BINS, 8, POINTS)


def list_space(slots):
    return pltpu.SMEM((slots * BLOCKS + BLOCKS + 3 * UNROLL,), jnp.int32)


def ghost_space(messages):
    slots = messages * SLOTS
    return (
        [pltpu.VMEM((slots * POINTS + STEP_ROWS, 8), jnp.float32)]
        + [list_space(slots)] * 4
        + [pltpu.SMEM((messages, 4, POINTS), jnp.float32), pltpu.SemaphoreType.DMA((2,))]
    )


def cost(microseconds):
    return pl.CostEstimate(flops=0, transcendentals=0, bytes_accessed=int(microseconds * 3.0e6))


def self_pairs(target, table):
    return pl.pallas_call(
        self_kernel,
        out_shape=[f32(*FORCE_SHAPE), f32(*COUNT_SHAPE)],
        in_specs=[VMEM, SMEM],
        out_specs=[VMEM] * 2,
        scratch_shapes=[pltpu.VMEM((CELLS * POINTS + STEP_ROWS, 8), jnp.float32)]
        + [list_space(CELLS)] * 2,
        compiler_params=PARAMS,
        cost_estimate=cost(6),
        name="self",
    )(target, table)


def near_pairs(target, table, from_even, from_odd, force, counts):
    return pl.pallas_call(
        near_kernel,
        out_shape=[f32(*FORCE_SHAPE), f32(*COUNT_SHAPE)],
        in_specs=[VMEM, SMEM] + [VMEM] * 4,
        out_specs=[VMEM] * 2,
        scratch_shapes=ghost_space(2),
        input_output_aliases={4: 0, 5: 1},
        compiler_params=PARAMS,
        cost_estimate=cost(4),
        name="near",
    )(target, table, from_even, from_odd, force, counts)


def far_pairs(devices, target, table, from_even, from_odd, force, counts):
    return pl.pallas_call(
        far_kernel,
        out_shape=[f32(*FORCE_SHAPE), f32(*COUNT_SHAPE), f32(*GRAD_SHAPE), f32(devices, 2, POINTS)],
        in_specs=[VMEM, SMEM] + [VMEM] * 4,
        out_specs=[VMEM] * 4,
        scratch_shapes=ghost_space(6),
        input_output_aliases={4: 0, 5: 1},
        compiler_params=PARAMS,
        cost_estimate=cost(12),
        name="far",
    )(target, table, from_even, from_odd, force, counts)[2:]


def body(positions, cell_points, target_log, export_count, export_cell, import_pair, import_shift):
    devices = export_count.shape[1]
    inputs = (
        positions, cell_points, target_log, export_count,
        jnp.transpose(export_cell, (2, 0, 1)),
        jnp.transpose(import_pair, (2, 0, 1)),
        jnp.transpose(import_shift, (0, 3, 1, 2)),
    )
    target, logs, table, *messages = pl.pallas_call(
        first_kernel,
        out_shape=[f32(*CELL_SHAPE), f32(BINS, POINTS), jax.ShapeDtypeStruct((TABLE,), jnp.int32)] + MESSAGES,
        in_specs=[pl.BlockSpec(memory_space=pltpu.HBM)] * 7,
        out_specs=[VMEM, VMEM, SMEM] + [VMEM] * 4,
        scratch_shapes=[
            pltpu.VMEM(positions.shape, jnp.float32),
            pltpu.SMEM(cell_points.shape, jnp.int32),
            pltpu.SMEM(target_log.shape, jnp.float32),
            pltpu.SMEM(export_count.shape, jnp.int32),
            pltpu.SMEM((SLOTS, 1, devices), jnp.int32),
            pltpu.SMEM((SLOTS, 1, devices), jnp.int32),
            pltpu.SMEM((3, SLOTS, 1, devices), jnp.int32),
            pltpu.VMEM(CELL_SHAPE, jnp.float32),
            pltpu.SemaphoreType.DMA((7,)),
        ],
        compiler_params=PARAMS,
        name="first",
    )(*(pltpu.with_memory_space_constraint(value, pltpu.HBM) for value in inputs))
    for iteration in range(STEPS):
        depth_even, depth_odd, sky_even, sky_odd = messages
        depth_even, depth_odd = swap(depth_even, "depth", 1), swap(depth_odd, "depth", 2)
        depth_even, depth_odd, force, counts = lax.optimization_barrier(
            (depth_even, depth_odd, *self_pairs(target, table))
        )
        near = near_pairs(target, table, depth_even, depth_odd, force, counts)
        sky_even = swap(jnp.stack([sky_even, depth_even[1], depth_odd[1]]), "sky", 1)
        sky_odd = swap(jnp.stack([sky_odd, depth_even[2], depth_odd[2]]), "sky", 2)
        grad, payload = far_pairs(devices, target, table, sky_even, sky_odd, *near)
        sums = lax.all_to_all(payload, AXES, 0, 0)
        if iteration == STEPS - 1:
            return pl.pallas_call(
                last_kernel,
                out_shape=f32(*positions.shape),
                in_specs=[VMEM] * 4,
                out_specs=VMEM,
                compiler_params=PARAMS,
                name="last",
            )(sums, grad, travel, logs)
        travel, target, *messages = pl.pallas_call(
            update_kernel,
            out_shape=[f32(*CELL_SHAPE), f32(*CELL_SHAPE)] + MESSAGES,
            in_specs=[VMEM] * 4 + [SMEM],
            out_specs=[VMEM] * 6,
            scratch_shapes=[pltpu.VMEM(CELL_SHAPE, jnp.float32)],
            compiler_params=PARAMS,
            name="update",
        )(sums, grad, target, logs, table)


def solution(mesh):
    in_specs = (
        P(None, ("sky", "depth"), None),
        P(("sky", "depth")),
        P(),
        P(("sky", "depth"), None),
        P(("sky", "depth"), None, None),
        P(("sky", "depth"), None, None),
        P(None, ("sky", "depth"), None, None),
    )
    out_specs = P(None, ("sky", "depth"), None)
    return jax.shard_map(body, mesh=mesh, in_specs=in_specs, out_specs=out_specs, check_vma=False)
```

```python
import functools
import math

import jax
import jax.numpy as jnp
from jax import lax
from jax.experimental import pallas as pl
from jax.experimental.pallas import tpu as pltpu
from jax.sharding import PartitionSpec as P

STEPS = 2
EPS_SQ = 0.0001
STEP_SIZE = 0.01

BINS = 16
CELLS = 16
POINTS = 128
SLOTS = 3
AXES = ("sky", "depth")

UNIT = math.sqrt(128.0 * math.log2(math.e))
CENTRES = [(b + 0.5) / 16.0 for b in range(BINS)]
CHAIN = 4
LIFT = 64.0
MIDDLE = CENTRES[8]
RADIUS_CAP = 2.1 * UNIT
FAR = 1.0e4
COUNT_SCALE = [
    math.exp(16.0 * (b % CHAIN) * (MIDDLE - CENTRES[b - b % CHAIN]) - 0.5 * (b % CHAIN) ** 2) * 2.0**-LIFT
    for b in range(BINS)
]
FORCE_SCALE = [-256.0 / UNIT * scale for scale in COUNT_SCALE]

NEIGHBOURS = [(1, 0), (2, 0), (0, 1), (1, 1), (2, 1), (0, 2), (1, 2), (2, 2)]
TABLE_ROW = 16
EXPORT, IMPORT, LIVE, SHIFT = 0, SLOTS, 2 * SLOTS, 2 * SLOTS + 1
SIZES = len(NEIGHBOURS) * TABLE_ROW
TABLE = SIZES + CELLS
STEP_ROWS = 16
BLOCKS = POINTS // STEP_ROWS
UNROLL = 4

VMEM = pl.BlockSpec(memory_space=pltpu.VMEM)
SMEM = pl.BlockSpec(memory_space=pltpu.SMEM)
PARAMS = pltpu.CompilerParams(vmem_limit_bytes=40 * 1024 * 1024)


def partner(axis, option):
    here = lax.axis_index(axis)
    if option == 0:
        return here
    step = 1 - 2 * (here % 2)
    return here + step if option == 1 else here - step


def neighbour(sky_option, depth_option):
    sky_count, depth_count = lax.axis_size("sky"), lax.axis_size("depth")
    sky = lax.rem(partner("sky", sky_option) + sky_count, sky_count)
    depth = partner("depth", depth_option)
    inside = (depth >= 0) & (depth < depth_count)
    return sky * depth_count + jnp.clip(depth, 0, depth_count - 1), inside


def column(values, shape):
    rows = lax.broadcasted_iota(jnp.int32, shape, 0)
    out = jnp.full(shape, values[0], jnp.float32)
    for index in range(1, len(values)):
        out = jnp.where(rows == index, values[index], out)
    return out


def shift_of(table, index, slot):
    rows = lax.broadcasted_iota(jnp.int32, (4, POINTS), 0)
    shift = jnp.zeros((4, POINTS), jnp.float32)
    for axis in range(3):
        amount = table[index * TABLE_ROW + SHIFT + axis * SLOTS + slot].astype(jnp.float32) * UNIT
        shift = jnp.where(rows == axis, amount, shift)
    return shift


def pack(source, table, outs):
    sky_even, sky_odd, depth_even, depth_odd = outs
    lanes = lax.broadcasted_iota(jnp.int32, (4, POINTS), 1)
    for index, (sky_option, depth_option) in enumerate(NEIGHBOURS):
        if sky_option == 0:
            out = depth_even if depth_option == 1 else depth_odd
        else:
            out = (sky_even if sky_option == 1 else sky_odd).at[depth_option]
        row = index * TABLE_ROW
        live = table[row + LIVE]
        meta = jnp.zeros((4, POINTS), jnp.float32)
        for slot in range(SLOTS):
            right = table[row + EXPORT + slot]
            out[slot] = source[right]
            size = jnp.where(slot < live, table[SIZES + right], 0)
            meta = jnp.where(lanes == slot, size.astype(jnp.float32), meta)
            left = table[row + IMPORT + slot]
            out[SLOTS + slot] = source[left] - shift_of(table, index, slot)
            size = table[SIZES + left]
            meta = jnp.where(lanes == SLOTS + slot, size.astype(jnp.float32), meta)
        out[2 * SLOTS] = meta


def first_kernel(
    positions_in, points_in, logs_in, count_in, export_in, import_in, shift_in,
    target, logs, table, sky_even, sky_odd, depth_even, depth_odd,
    positions, points, log_list, count, exports, imports, shifts, source, sems,
):
    pairs = [
        (points_in, points), (count_in, count), (export_in, exports), (import_in, imports),
        (shift_in, shifts), (positions_in, positions), (logs_in, log_list),
    ]
    copies = [
        pltpu.make_async_copy(origin, place, sems.at[index])
        for index, (origin, place) in enumerate(pairs)
    ]
    for copy in copies:
        copy.start()
    for copy in copies:
        copy.wait()
    for cell in range(CELLS):
        table[SIZES + cell] = points[cell]
    for index, options in enumerate(NEIGHBOURS):
        device, inside = neighbour(*options)
        row = index * TABLE_ROW
        table[row + LIVE] = jnp.where(inside, count[0, device], 0)
        for slot in range(SLOTS):
            table[row + EXPORT + slot] = exports[slot, 0, device]
            table[row + IMPORT + slot] = imports[slot, 0, device]
            for axis in range(3):
                table[row + SHIFT + axis * SLOTS + slot] = shifts[axis, slot, 0, device]
    logs[...] = column([log_list[b] for b in range(BINS)], (BINS, POINTS))
    lanes = lax.broadcasted_iota(jnp.int32, (4, POINTS), 1)
    for cell in range(CELLS):
        rows = [positions[axis, cell : cell + 1, :] for axis in range(3)]
        tile = jnp.concatenate(rows + [jnp.zeros((1, POINTS), jnp.float32)], axis=0) * UNIT
        live = lanes < points[cell]
        target[cell] = jnp.where(live, tile, -FAR)
        source[cell] = jnp.where(live, tile, FAR)
    pack(source, table, (sky_even, sky_odd, depth_even, depth_odd))


def shape_pairs(at, row_list, cell_list, source, base, target):
    units = range(UNROLL)
    blocks = [
        source[pl.ds(pl.multiple_of(row_list[at + unit] * STEP_ROWS, STEP_ROWS), STEP_ROWS), :]
        for unit in units
    ]
    spread = [
        [
            jnp.broadcast_to(blocks[unit][:, base + axis : base + axis + 1], (STEP_ROWS, POINTS))
            for unit in units
        ]
        for axis in range(3)
    ]
    out = []
    for unit in units:
        cell = cell_list[at + unit]
        dx, dy, dz = (target[cell, axis : axis + 1, :] - spread[axis][unit] for axis in range(3))
        square = dx * dx + dy * dy + dz * dz + EPS_SQ * UNIT * UNIT
        inverse = lax.rsqrt(square)
        radius = jnp.minimum(square * inverse, RADIUS_CAP)
        ratio = jnp.exp2(
            radius * (16.0 * math.log2(math.e) / UNIT) - 16.0 * math.log2(math.e) * MIDDLE
        )
        out.append((radius, ratio, dx * inverse, dy * inverse, dz * inverse))
    return out


def add_block(values, cell, force, counts):
    radius, ratio, *units = values
    for chain in range(BINS // CHAIN):
        for link in range(CHAIN):
            b = chain * CHAIN + link
            delta = radius - CENTRES[b] * UNIT
            if link == 0:
                value = jnp.exp2(LIFT - delta * delta)
            else:
                value = value * ratio
            if counts is not None:
                counts[b] += value[:8] + value[8:]
            slope = value * delta
            for axis in range(3):
                pulled = slope * units[axis]
                force[cell, axis * BINS + b] += pulled[:8] + pulled[8:]


def add_blocks(total, row_list, cell_list, base, target, source, force, counts):
    def step(turn, shapes):
        at = turn * UNROLL
        ahead = shape_pairs(at + UNROLL, row_list, cell_list, source, base, target)
        for unit in range(UNROLL):
            add_block(shapes[unit], cell_list[at + unit], force, counts)
        return ahead

    first = shape_pairs(0, row_list, cell_list, source, base, target)
    lax.fori_loop(0, (total + (UNROLL - 1)) // UNROLL, step, first)


def list_blocks(at, slot, cell, size, row_list, cell_list):
    for block in range(BLOCKS):
        row_list[at + block] = slot * BLOCKS + block
        cell_list[at + block] = cell
    return at + (size + (STEP_ROWS - 1)) // STEP_ROWS


def end_list(at, slots, row_list, cell_list):
    for spare in range(3 * UNROLL):
        row_list[at + spare] = slots * BLOCKS
        cell_list[at + spare] = 0


def put_points(source, slot, first, second):
    source[slot * POINTS : (slot + 1) * POINTS] = jnp.transpose(
        jnp.concatenate([first, second], axis=0), (1, 0)
    )


def self_kernel(target, table, force, counts, source, row_list, cell_list):
    lanes = lax.broadcasted_iota(jnp.int32, (4, POINTS), 1)
    end = 0
    for cell in range(CELLS):
        size = table[SIZES + cell]
        tile = jnp.where(lanes < size, target[cell], FAR)
        put_points(source, cell, tile, tile)
        end = list_blocks(end, cell, cell, size, row_list, cell_list)
    end_list(end, CELLS, row_list, cell_list)
    source[CELLS * POINTS :] = jnp.full((STEP_ROWS, 8), FAR, jnp.float32)
    force[...] = jnp.zeros(force.shape, jnp.float32)
    counts[...] = jnp.zeros(counts.shape, jnp.float32)
    add_blocks(end, row_list, cell_list, 0, target, source, force, counts)
    counts[...] = 0.5 * counts[...]


def ghost_pairs(
    messages, metas, first, target, table, force, counts,
    source, import_rows, import_cells, export_rows, export_cells, meta, sems,
):
    copies = []
    at = 0
    for index, part in enumerate(metas):
        size = part.shape[0]
        copies.append(pltpu.make_async_copy(part, meta.at[at : at + size], sems.at[index]))
        at += size
    for copy in copies:
        copy.start()
    for index, message in enumerate(messages):
        for slot in range(SLOTS):
            put_points(
                source, index * SLOTS + slot,
                message[slot] + shift_of(table, first + index, slot), message[SLOTS + slot],
            )
    slots = len(messages) * SLOTS
    source[slots * POINTS :] = jnp.full((STEP_ROWS, 8), FAR, jnp.float32)
    for copy in copies:
        copy.wait()
    import_end = 0
    export_end = 0
    for index in range(len(messages)):
        row = (first + index) * TABLE_ROW
        live = table[row + LIVE]
        for slot in range(SLOTS):
            at = index * SLOTS + slot
            size = meta[index, 0, slot].astype(jnp.int32)
            import_end = list_blocks(
                import_end, at, table[row + IMPORT + slot], size, import_rows, import_cells
            )
            size = jnp.where(slot < live, meta[index, 0, SLOTS + slot].astype(jnp.int32), 0)
            export_end = list_blocks(
                export_end, at, table[row + EXPORT + slot], size, export_rows, export_cells
            )
    end_list(import_end, slots, import_rows, import_cells)
    end_list(export_end, slots, export_rows, export_cells)
    add_blocks(
        import_end, import_rows, import_cells, 0, target, source, force, counts
    )
    add_blocks(
        export_end, export_rows, export_cells, 4, target, source, force, None
    )


def near_kernel(target, table, from_even, from_odd, force_in, counts_in, force, counts, *scratch):
    ghost_pairs(
        [from_even.at[0], from_odd.at[0]],
        [side.at[0:1, 2 * SLOTS] for side in (from_even, from_odd)],
        0, target, table, force, counts, *scratch,
    )


def far_kernel(
    target, table, from_even, from_odd, force_in, counts_in, force, counts, grad, payload, *scratch,
):
    ghost_pairs(
        [side.at[index] for side in (from_even, from_odd) for index in range(3)],
        [side.at[:, 2 * SLOTS] for side in (from_even, from_odd)],
        2, target, table, force, counts, *scratch,
    )
    force_scale = column(FORCE_SCALE, (BINS, POINTS))
    for cell in range(CELLS):
        for axis in range(3):
            tile = jnp.sum(force[cell, axis * BINS : (axis + 1) * BINS], axis=1) * force_scale
            at = (cell * 3 + axis) * POINTS
            grad[:, at : at + POINTS] = tile
    whole = grad[...]
    gram = lax.dot_general(
        whole, whole, (((1,), (1,)), ((), ())),
        precision=lax.Precision.HIGHEST, preferred_element_type=jnp.float32,
    )
    bins = lax.broadcasted_iota(jnp.int32, (BINS, POINTS), 0)
    lane = lax.broadcasted_iota(jnp.int32, (BINS, POINTS), 1)
    low, high = lane % BINS, lane // BINS
    spread = jnp.where(low == bins, 1.0, 0.0)
    wide = lax.dot_general(
        gram, spread, (((1,), (0,)), ((), ())),
        precision=lax.Precision.HIGHEST, preferred_element_type=jnp.float32,
    )
    first = jnp.sum(jnp.where(bins == (low + high) % BINS, wide, 0.0), axis=0, keepdims=True)
    second = jnp.where((bins == (low + 8) % BINS) & (high == 0), wide, 0.0)
    sums = jnp.sum(counts[...], axis=1)
    sums = jnp.sum(sums, axis=1, keepdims=True) * column(COUNT_SCALE, (BINS, POINTS))
    second = second + jnp.where(lane == bins + BINS, sums, 0.0)
    total = table[SIZES]
    for cell in range(1, CELLS):
        total = total + table[SIZES + cell]
    second = second + jnp.where((lane == 2 * BINS) & (bins == 0), total.astype(jnp.float32), 0.0)
    second = jnp.sum(second, axis=0, keepdims=True)
    both = jnp.concatenate([first, second], axis=0)
    payload[...] = jnp.broadcast_to(both[None], payload.shape)


def moves_of(sums, grad, logs):
    both = jnp.sum(sums[...], axis=0)
    bins = lax.broadcasted_iota(jnp.int32, (BINS, POINTS), 0)
    lane = lax.broadcasted_iota(jnp.int32, (BINS, POINTS), 1)
    low, high = lane % BINS, lane // BINS
    first, second = both[0:1], both[1:2]
    counts = jnp.sum(
        jnp.where(lane == bins + BINS, jnp.broadcast_to(second, (BINS, POINTS)), 0.0), axis=1, keepdims=True
    )
    counts = jnp.broadcast_to(counts, (BINS, POINTS))
    one_lane = lax.broadcasted_iota(jnp.int32, (1, POINTS), 1)
    valid = jnp.sum(jnp.where(one_lane == 2 * BINS, second, 0.0), axis=1, keepdims=True)
    mean_count = jnp.sum(counts, axis=0, keepdims=True) / BINS
    pull = (jnp.log(1.0 + counts) - logs[...]) * mean_count / (1.0 + counts)
    here = jnp.sum(jnp.where(bins == low, pull, 0.0), axis=0, keepdims=True)
    there = jnp.sum(jnp.where(bins == (low + high) % BINS, pull, 0.0), axis=0, keepdims=True)
    across = jnp.sum(jnp.where(bins == (low + 8) % BINS, pull, 0.0), axis=0, keepdims=True)
    power = first * here * there * jnp.where(one_lane < BINS, 1.0, 2.0)
    power = power + jnp.where(one_lane < BINS, second * here * across, 0.0)
    power = jnp.maximum(jnp.sum(power, axis=1, keepdims=True), 0.0)
    rms = jnp.sqrt(power / (3.0 * valid) + 1e-06)
    weights = pull / -rms
    out = []
    for cell in range(CELLS):
        parts = []
        for axis in range(3):
            at = (cell * 3 + axis) * POINTS
            parts.append(jnp.sum(grad[:, at : at + POINTS] * weights, axis=0, keepdims=True))
        out.append(parts)
    return out


def update_kernel(
    sums, grad, target, logs, table,
    travel, next_target, sky_even, sky_odd, depth_even, depth_odd, source,
):
    lanes = lax.broadcasted_iota(jnp.int32, (4, POINTS), 1)
    moves = moves_of(sums, grad, logs)
    for cell in range(CELLS):
        tile = jnp.concatenate(moves[cell] + [jnp.zeros((1, POINTS), jnp.float32)], axis=0)
        travel[cell] = tile
        tile = target[cell] + (STEP_SIZE * UNIT) * tile
        next_target[cell] = tile
        source[cell] = jnp.where(lanes < table[SIZES + cell], tile, FAR)
    pack(source, table, (sky_even, sky_odd, depth_even, depth_odd))


def last_kernel(sums, grad, travel, logs, out):
    moves = moves_of(sums, grad, logs)
    for cell in range(CELLS):
        for axis in range(3):
            out[axis, cell : cell + 1, :] = travel[cell, axis : axis + 1, :] + moves[cell][axis]


def f32(*shape):
    return jax.ShapeDtypeStruct(shape, jnp.float32)


CELL_SHAPE = (CELLS, 4, POINTS)
GRAD_SHAPE = (BINS, CELLS * 3 * POINTS)
MESSAGE = (2 * SLOTS + 1, 4, POINTS)
MESSAGES = [f32(3, *MESSAGE), f32(3, *MESSAGE), f32(*MESSAGE), f32(*MESSAGE)]


def swap(value, axis, option):
    count = lax.axis_size(axis)
    perm = []
    for low in range(option - 1, count, 2):
        high = low + 1
        if high < count or axis == "sky":
            perm += [(low, high % count), (high % count, low)]
    return lax.ppermute(value, axis, perm)


FORCE_SHAPE = (CELLS, 3 * BINS, 8, POINTS)
COUNT_SHAPE = (BINS, 8, POINTS)


def list_space(slots):
    return pltpu.SMEM((slots * BLOCKS + BLOCKS + 3 * UNROLL,), jnp.int32)


def ghost_space(messages):
    slots = messages * SLOTS
    return (
        [pltpu.VMEM((slots * POINTS + STEP_ROWS, 8), jnp.float32)]
        + [list_space(slots)] * 4
        + [pltpu.SMEM((messages, 4, POINTS), jnp.float32), pltpu.SemaphoreType.DMA((2,))]
    )


def cost(microseconds):
    return pl.CostEstimate(flops=0, transcendentals=0, bytes_accessed=int(microseconds * 3.0e6))


def self_pairs(target, table):
    return pl.pallas_call(
        self_kernel,
        out_shape=[f32(*FORCE_SHAPE), f32(*COUNT_SHAPE)],
        in_specs=[VMEM, SMEM],
        out_specs=[VMEM] * 2,
        scratch_shapes=[pltpu.VMEM((CELLS * POINTS + STEP_ROWS, 8), jnp.float32)]
        + [list_space(CELLS)] * 2,
        compiler_params=PARAMS,
        cost_estimate=cost(6),
        name="self",
    )(target, table)


def near_pairs(target, table, from_even, from_odd, force, counts):
    return pl.pallas_call(
        near_kernel,
        out_shape=[f32(*FORCE_SHAPE), f32(*COUNT_SHAPE)],
        in_specs=[VMEM, SMEM] + [VMEM] * 4,
        out_specs=[VMEM] * 2,
        scratch_shapes=ghost_space(2),
        input_output_aliases={4: 0, 5: 1},
        compiler_params=PARAMS,
        cost_estimate=cost(4),
        name="near",
    )(target, table, from_even, from_odd, force, counts)


def far_pairs(devices, target, table, from_even, from_odd, force, counts):
    return pl.pallas_call(
        far_kernel,
        out_shape=[f32(*FORCE_SHAPE), f32(*COUNT_SHAPE), f32(*GRAD_SHAPE), f32(devices, 2, POINTS)],
        in_specs=[VMEM, SMEM] + [VMEM] * 4,
        out_specs=[VMEM] * 4,
        scratch_shapes=ghost_space(6),
        input_output_aliases={4: 0, 5: 1},
        compiler_params=PARAMS,
        cost_estimate=cost(12),
        name="far",
    )(target, table, from_even, from_odd, force, counts)[2:]


def body(positions, cell_points, target_log, export_count, export_cell, import_pair, import_shift):
    devices = export_count.shape[1]
    inputs = (
        positions, cell_points, target_log, export_count,
        jnp.transpose(export_cell, (2, 0, 1)),
        jnp.transpose(import_pair, (2, 0, 1)),
        jnp.transpose(import_shift, (0, 3, 1, 2)),
    )
    target, logs, table, *messages = pl.pallas_call(
        first_kernel,
        out_shape=[f32(*CELL_SHAPE), f32(BINS, POINTS), jax.ShapeDtypeStruct((TABLE,), jnp.int32)] + MESSAGES,
        in_specs=[pl.BlockSpec(memory_space=pltpu.HBM)] * 7,
        out_specs=[VMEM, VMEM, SMEM] + [VMEM] * 4,
        scratch_shapes=[
            pltpu.VMEM(positions.shape, jnp.float32),
            pltpu.SMEM(cell_points.shape, jnp.int32),
            pltpu.SMEM(target_log.shape, jnp.float32),
            pltpu.SMEM(export_count.shape, jnp.int32),
            pltpu.SMEM((SLOTS, 1, devices), jnp.int32),
            pltpu.SMEM((SLOTS, 1, devices), jnp.int32),
            pltpu.SMEM((3, SLOTS, 1, devices), jnp.int32),
            pltpu.VMEM(CELL_SHAPE, jnp.float32),
            pltpu.SemaphoreType.DMA((7,)),
        ],
        compiler_params=PARAMS,
        name="first",
    )(*(pltpu.with_memory_space_constraint(value, pltpu.HBM) for value in inputs))
    for iteration in range(STEPS):
        sky_even, sky_odd, depth_even, depth_odd = messages
        sky_even, sky_odd = swap(sky_even, "sky", 1), swap(sky_odd, "sky", 2)
        sky_even, sky_odd, force, counts = lax.optimization_barrier(
            (sky_even, sky_odd, *self_pairs(target, table))
        )
        near = near_pairs(target, table, sky_even, sky_odd, force, counts)
        depth_even = swap(jnp.stack([depth_even, sky_even[1], sky_odd[1]]), "depth", 1)
        depth_odd = swap(jnp.stack([depth_odd, sky_even[2], sky_odd[2]]), "depth", 2)
        grad, payload = far_pairs(devices, target, table, depth_even, depth_odd, *near)
        sums = lax.all_to_all(payload, AXES, 0, 0)
        if iteration == STEPS - 1:
            return pl.pallas_call(
                last_kernel,
                out_shape=f32(*positions.shape),
                in_specs=[VMEM] * 4,
                out_specs=VMEM,
                compiler_params=PARAMS,
                name="last",
            )(sums, grad, travel, logs)
        travel, target, *messages = pl.pallas_call(
            update_kernel,
            out_shape=[f32(*CELL_SHAPE), f32(*CELL_SHAPE)] + MESSAGES,
            in_specs=[VMEM] * 4 + [SMEM],
            out_specs=[VMEM] * 6,
            scratch_shapes=[pltpu.VMEM(CELL_SHAPE, jnp.float32)],
            compiler_params=PARAMS,
            name="update",
        )(sums, grad, target, logs, table)


def solution(mesh):
    in_specs = (
        P(None, ("sky", "depth"), None),
        P(("sky", "depth")),
        P(),
        P(("sky", "depth"), None),
        P(("sky", "depth"), None, None),
        P(("sky", "depth"), None, None),
        P(None, ("sky", "depth"), None, None),
    )
    out_specs = P(None, ("sky", "depth"), None)
    return jax.shard_map(body, mesh=mesh, in_specs=in_specs, out_specs=out_specs, check_vma=False)
```

```python
import functools
import math

import jax
import jax.numpy as jnp
from jax import lax
from jax.experimental import pallas as pl
from jax.experimental.pallas import tpu as pltpu
from jax.sharding import PartitionSpec as P

STEPS = 2
EPS_SQ = 0.0001
STEP_SIZE = 0.01

BINS = 16
CELLS = 16
POINTS = 128
SLOTS = 3
AXES = ("sky", "depth")

UNIT = math.sqrt(128.0 * math.log2(math.e))
CENTRES = [(b + 0.5) / 16.0 for b in range(BINS)]
CHAIN = 4
LIFT = 64.0
MIDDLE = CENTRES[8]
RADIUS_CAP = 2.1 * UNIT
FAR = 1.0e4
COUNT_SCALE = [
    math.exp(16.0 * (b % CHAIN) * (MIDDLE - CENTRES[b - b % CHAIN]) - 0.5 * (b % CHAIN) ** 2) * 2.0**-LIFT
    for b in range(BINS)
]
FORCE_SCALE = [-256.0 / UNIT * scale for scale in COUNT_SCALE]

NEIGHBOURS = [(1, 0), (2, 0), (0, 1), (1, 1), (2, 1), (0, 2), (1, 2), (2, 2)]
TABLE_ROW = 16
EXPORT, IMPORT, LIVE, SHIFT = 0, SLOTS, 2 * SLOTS, 2 * SLOTS + 1
SIZES = len(NEIGHBOURS) * TABLE_ROW
TABLE = SIZES + CELLS
STEP_ROWS = 16
BLOCKS = POINTS // STEP_ROWS
UNROLL = 3

VMEM = pl.BlockSpec(memory_space=pltpu.VMEM)
SMEM = pl.BlockSpec(memory_space=pltpu.SMEM)
PARAMS = pltpu.CompilerParams(vmem_limit_bytes=40 * 1024 * 1024)


def partner(axis, option):
    here = lax.axis_index(axis)
    if option == 0:
        return here
    step = 1 - 2 * (here % 2)
    return here + step if option == 1 else here - step


def neighbour(sky_option, depth_option):
    sky_count, depth_count = lax.axis_size("sky"), lax.axis_size("depth")
    sky = lax.rem(partner("sky", sky_option) + sky_count, sky_count)
    depth = partner("depth", depth_option)
    inside = (depth >= 0) & (depth < depth_count)
    return sky * depth_count + jnp.clip(depth, 0, depth_count - 1), inside


def column(values, shape):
    rows = lax.broadcasted_iota(jnp.int32, shape, 0)
    out = jnp.full(shape, values[0], jnp.float32)
    for index in range(1, len(values)):
        out = jnp.where(rows == index, values[index], out)
    return out


def shift_of(table, index, slot):
    rows = lax.broadcasted_iota(jnp.int32, (4, POINTS), 0)
    shift = jnp.zeros((4, POINTS), jnp.float32)
    for axis in range(3):
        amount = table[index * TABLE_ROW + SHIFT + axis * SLOTS + slot].astype(jnp.float32) * UNIT
        shift = jnp.where(rows == axis, amount, shift)
    return shift


def pack(source, table, outs):
    sky_even, sky_odd, depth_even, depth_odd = outs
    lanes = lax.broadcasted_iota(jnp.int32, (4, POINTS), 1)
    for index, (sky_option, depth_option) in enumerate(NEIGHBOURS):
        if sky_option == 0:
            out = depth_even if depth_option == 1 else depth_odd
        else:
            out = (sky_even if sky_option == 1 else sky_odd).at[depth_option]
        row = index * TABLE_ROW
        live = table[row + LIVE]
        meta = jnp.zeros((4, POINTS), jnp.float32)
        for slot in range(SLOTS):
            right = table[row + EXPORT + slot]
            out[slot] = source[right]
            size = jnp.where(slot < live, table[SIZES + right], 0)
            meta = jnp.where(lanes == slot, size.astype(jnp.float32), meta)
            left = table[row + IMPORT + slot]
            out[SLOTS + slot] = source[left] - shift_of(table, index, slot)
            size = table[SIZES + left]
            meta = jnp.where(lanes == SLOTS + slot, size.astype(jnp.float32), meta)
        out[2 * SLOTS] = meta


def first_kernel(
    positions_in, points_in, logs_in, count_in, export_in, import_in, shift_in,
    target, logs, table, sky_even, sky_odd, depth_even, depth_odd,
    positions, points, log_list, count, exports, imports, shifts, source, sems,
):
    pairs = [
        (points_in, points), (count_in, count), (export_in, exports), (import_in, imports),
        (shift_in, shifts), (positions_in, positions), (logs_in, log_list),
    ]
    copies = [
        pltpu.make_async_copy(origin, place, sems.at[index])
        for index, (origin, place) in enumerate(pairs)
    ]
    for copy in copies:
        copy.start()
    for copy in copies:
        copy.wait()
    for cell in range(CELLS):
        table[SIZES + cell] = points[cell]
    for index, options in enumerate(NEIGHBOURS):
        device, inside = neighbour(*options)
        row = index * TABLE_ROW
        table[row + LIVE] = jnp.where(inside, count[0, device], 0)
        for slot in range(SLOTS):
            table[row + EXPORT + slot] = exports[slot, 0, device]
            table[row + IMPORT + slot] = imports[slot, 0, device]
            for axis in range(3):
                table[row + SHIFT + axis * SLOTS + slot] = shifts[axis, slot, 0, device]
    logs[...] = column([log_list[b] for b in range(BINS)], (BINS, POINTS))
    lanes = lax.broadcasted_iota(jnp.int32, (4, POINTS), 1)
    for cell in range(CELLS):
        rows = [positions[axis, cell : cell + 1, :] for axis in range(3)]
        tile = jnp.concatenate(rows + [jnp.zeros((1, POINTS), jnp.float32)], axis=0) * UNIT
        live = lanes < points[cell]
        target[cell] = jnp.where(live, tile, -FAR)
        source[cell] = jnp.where(live, tile, FAR)
    pack(source, table, (sky_even, sky_odd, depth_even, depth_odd))


def shape_pairs(at, row_list, cell_list, source, base, target):
    units = range(UNROLL)
    blocks = [
        source[pl.ds(pl.multiple_of(row_list[at + unit] * STEP_ROWS, STEP_ROWS), STEP_ROWS), :]
        for unit in units
    ]
    spread = [
        [
            jnp.broadcast_to(blocks[unit][:, base + axis : base + axis + 1], (STEP_ROWS, POINTS))
            for unit in units
        ]
        for axis in range(3)
    ]
    out = []
    for unit in units:
        cell = cell_list[at + unit]
        dx, dy, dz = (target[cell, axis : axis + 1, :] - spread[axis][unit] for axis in range(3))
        square = dx * dx + dy * dy + dz * dz + EPS_SQ * UNIT * UNIT
        inverse = lax.rsqrt(square)
        radius = jnp.minimum(square * inverse, RADIUS_CAP)
        ratio = jnp.exp2(
            radius * (16.0 * math.log2(math.e) / UNIT) - 16.0 * math.log2(math.e) * MIDDLE
        )
        out.append((radius, ratio, dx * inverse, dy * inverse, dz * inverse))
    return out


def add_block(values, cell, force, counts):
    radius, ratio, *units = values
    for chain in range(BINS // CHAIN):
        for link in range(CHAIN):
            b = chain * CHAIN + link
            delta = radius - CENTRES[b] * UNIT
            if link == 0:
                value = jnp.exp2(LIFT - delta * delta)
            else:
                value = value * ratio
            if counts is not None:
                counts[b] += value[:8] + value[8:]
            slope = value * delta
            for axis in range(3):
                pulled = slope * units[axis]
                force[cell, axis * BINS + b] += pulled[:8] + pulled[8:]


def add_blocks(total, row_list, cell_list, base, target, source, force, counts):
    def step(turn, shapes):
        at = turn * UNROLL
        ahead = shape_pairs(at + UNROLL, row_list, cell_list, source, base, target)
        for unit in range(UNROLL):
            add_block(shapes[unit], cell_list[at + unit], force, counts)
        return ahead

    first = shape_pairs(0, row_list, cell_list, source, base, target)
    lax.fori_loop(0, (total + (UNROLL - 1)) // UNROLL, step, first)


def list_blocks(at, slot, cell, size, row_list, cell_list):
    for block in range(BLOCKS):
        row_list[at + block] = slot * BLOCKS + block
        cell_list[at + block] = cell
    return at + (size + (STEP_ROWS - 1)) // STEP_ROWS


def end_list(at, slots, row_list, cell_list):
    for spare in range(3 * UNROLL):
        row_list[at + spare] = slots * BLOCKS
        cell_list[at + spare] = 0


def put_points(source, slot, first, second):
    source[slot * POINTS : (slot + 1) * POINTS] = jnp.transpose(
        jnp.concatenate([first, second], axis=0), (1, 0)
    )


def self_kernel(target, table, force, counts, source, row_list, cell_list):
    lanes = lax.broadcasted_iota(jnp.int32, (4, POINTS), 1)
    end = 0
    for cell in range(CELLS):
        size = table[SIZES + cell]
        tile = jnp.where(lanes < size, target[cell], FAR)
        put_points(source, cell, tile, tile)
        end = list_blocks(end, cell, cell, size, row_list, cell_list)
    end_list(end, CELLS, row_list, cell_list)
    source[CELLS * POINTS :] = jnp.full((STEP_ROWS, 8), FAR, jnp.float32)
    force[...] = jnp.zeros(force.shape, jnp.float32)
    counts[...] = jnp.zeros(counts.shape, jnp.float32)
    add_blocks(end, row_list, cell_list, 0, target, source, force, counts)
    counts[...] = 0.5 * counts[...]


def ghost_pairs(
    messages, metas, first, target, table, force, counts,
    source, import_rows, import_cells, export_rows, export_cells, meta, sems,
):
    copies = []
    at = 0
    for index, part in enumerate(metas):
        size = part.shape[0]
        copies.append(pltpu.make_async_copy(part, meta.at[at : at + size], sems.at[index]))
        at += size
    for copy in copies:
        copy.start()
    for index, message in enumerate(messages):
        for slot in range(SLOTS):
            put_points(
                source, index * SLOTS + slot,
                message[slot] + shift_of(table, first + index, slot), message[SLOTS + slot],
            )
    slots = len(messages) * SLOTS
    source[slots * POINTS :] = jnp.full((STEP_ROWS, 8), FAR, jnp.float32)
    for copy in copies:
        copy.wait()
    import_end = 0
    export_end = 0
    for index in range(len(messages)):
        row = (first + index) * TABLE_ROW
        live = table[row + LIVE]
        for slot in range(SLOTS):
            at = index * SLOTS + slot
            size = meta[index, 0, slot].astype(jnp.int32)
            import_end = list_blocks(
                import_end, at, table[row + IMPORT + slot], size, import_rows, import_cells
            )
            size = jnp.where(slot < live, meta[index, 0, SLOTS + slot].astype(jnp.int32), 0)
            export_end = list_blocks(
                export_end, at, table[row + EXPORT + slot], size, export_rows, export_cells
            )
    end_list(import_end, slots, import_rows, import_cells)
    end_list(export_end, slots, export_rows, export_cells)
    add_blocks(
        import_end, import_rows, import_cells, 0, target, source, force, counts
    )
    add_blocks(
        export_end, export_rows, export_cells, 4, target, source, force, None
    )


def near_kernel(target, table, from_even, from_odd, force_in, counts_in, force, counts, *scratch):
    ghost_pairs(
        [from_even.at[0], from_odd.at[0]],
        [side.at[0:1, 2 * SLOTS] for side in (from_even, from_odd)],
        0, target, table, force, counts, *scratch,
    )


def far_kernel(
    target, table, from_even, from_odd, force_in, counts_in, force, counts, grad, payload, *scratch,
):
    ghost_pairs(
        [side.at[index] for side in (from_even, from_odd) for index in range(3)],
        [side.at[:, 2 * SLOTS] for side in (from_even, from_odd)],
        2, target, table, force, counts, *scratch,
    )
    force_scale = column(FORCE_SCALE, (BINS, POINTS))
    for cell in range(CELLS):
        for axis in range(3):
            tile = jnp.sum(force[cell, axis * BINS : (axis + 1) * BINS], axis=1) * force_scale
            at = (cell * 3 + axis) * POINTS
            grad[:, at : at + POINTS] = tile
    whole = grad[...]
    gram = lax.dot_general(
        whole, whole, (((1,), (1,)), ((), ())),
        precision=lax.Precision.HIGHEST, preferred_element_type=jnp.float32,
    )
    bins = lax.broadcasted_iota(jnp.int32, (BINS, POINTS), 0)
    lane = lax.broadcasted_iota(jnp.int32, (BINS, POINTS), 1)
    low, high = lane % BINS, lane // BINS
    spread = jnp.where(low == bins, 1.0, 0.0)
    wide = lax.dot_general(
        gram, spread, (((1,), (0,)), ((), ())),
        precision=lax.Precision.HIGHEST, preferred_element_type=jnp.float32,
    )
    first = jnp.sum(jnp.where(bins == (low + high) % BINS, wide, 0.0), axis=0, keepdims=True)
    second = jnp.where((bins == (low + 8) % BINS) & (high == 0), wide, 0.0)
    sums = jnp.sum(counts[...], axis=1)
    sums = jnp.sum(sums, axis=1, keepdims=True) * column(COUNT_SCALE, (BINS, POINTS))
    second = second + jnp.where(lane == bins + BINS, sums, 0.0)
    total = table[SIZES]
    for cell in range(1, CELLS):
        total = total + table[SIZES + cell]
    second = second + jnp.where((lane == 2 * BINS) & (bins == 0), total.astype(jnp.float32), 0.0)
    second = jnp.sum(second, axis=0, keepdims=True)
    both = jnp.concatenate([first, second], axis=0)
    payload[...] = jnp.broadcast_to(both[None], payload.shape)


def moves_of(sums, grad, logs):
    both = jnp.sum(sums[...], axis=0)
    bins = lax.broadcasted_iota(jnp.int32, (BINS, POINTS), 0)
    lane = lax.broadcasted_iota(jnp.int32, (BINS, POINTS), 1)
    low, high = lane % BINS, lane // BINS
    first, second = both[0:1], both[1:2]
    counts = jnp.sum(
        jnp.where(lane == bins + BINS, jnp.broadcast_to(second, (BINS, POINTS)), 0.0), axis=1, keepdims=True
    )
    counts = jnp.broadcast_to(counts, (BINS, POINTS))
    one_lane = lax.broadcasted_iota(jnp.int32, (1, POINTS), 1)
    valid = jnp.sum(jnp.where(one_lane == 2 * BINS, second, 0.0), axis=1, keepdims=True)
    mean_count = jnp.sum(counts, axis=0, keepdims=True) / BINS
    pull = (jnp.log(1.0 + counts) - logs[...]) * mean_count / (1.0 + counts)
    here = jnp.sum(jnp.where(bins == low, pull, 0.0), axis=0, keepdims=True)
    there = jnp.sum(jnp.where(bins == (low + high) % BINS, pull, 0.0), axis=0, keepdims=True)
    across = jnp.sum(jnp.where(bins == (low + 8) % BINS, pull, 0.0), axis=0, keepdims=True)
    power = first * here * there * jnp.where(one_lane < BINS, 1.0, 2.0)
    power = power + jnp.where(one_lane < BINS, second * here * across, 0.0)
    power = jnp.maximum(jnp.sum(power, axis=1, keepdims=True), 0.0)
    rms = jnp.sqrt(power / (3.0 * valid) + 1e-06)
    weights = pull / -rms
    out = []
    for cell in range(CELLS):
        parts = []
        for axis in range(3):
            at = (cell * 3 + axis) * POINTS
            parts.append(jnp.sum(grad[:, at : at + POINTS] * weights, axis=0, keepdims=True))
        out.append(parts)
    return out


def update_kernel(
    sums, grad, target, logs, table,
    travel, next_target, sky_even, sky_odd, depth_even, depth_odd, source,
):
    lanes = lax.broadcasted_iota(jnp.int32, (4, POINTS), 1)
    moves = moves_of(sums, grad, logs)
    for cell in range(CELLS):
        tile = jnp.concatenate(moves[cell] + [jnp.zeros((1, POINTS), jnp.float32)], axis=0)
        travel[cell] = tile
        tile = target[cell] + (STEP_SIZE * UNIT) * tile
        next_target[cell] = tile
        source[cell] = jnp.where(lanes < table[SIZES + cell], tile, FAR)
    pack(source, table, (sky_even, sky_odd, depth_even, depth_odd))


def last_kernel(sums, grad, travel, logs, out):
    moves = moves_of(sums, grad, logs)
    for cell in range(CELLS):
        for axis in range(3):
            out[axis, cell : cell + 1, :] = travel[cell, axis : axis + 1, :] + moves[cell][axis]


def f32(*shape):
    return jax.ShapeDtypeStruct(shape, jnp.float32)


CELL_SHAPE = (CELLS, 4, POINTS)
GRAD_SHAPE = (BINS, CELLS * 3 * POINTS)
MESSAGE = (2 * SLOTS + 1, 4, POINTS)
MESSAGES = [f32(3, *MESSAGE), f32(3, *MESSAGE), f32(*MESSAGE), f32(*MESSAGE)]


def swap(value, axis, option):
    count = lax.axis_size(axis)
    perm = []
    for low in range(option - 1, count, 2):
        high = low + 1
        if high < count or axis == "sky":
            perm += [(low, high % count), (high % count, low)]
    return lax.ppermute(value, axis, perm)


FORCE_SHAPE = (CELLS, 3 * BINS, 8, POINTS)
COUNT_SHAPE = (BINS, 8, POINTS)


def list_space(slots):
    return pltpu.SMEM((slots * BLOCKS + BLOCKS + 3 * UNROLL,), jnp.int32)


def ghost_space(messages):
    slots = messages * SLOTS
    return (
        [pltpu.VMEM((slots * POINTS + STEP_ROWS, 8), jnp.float32)]
        + [list_space(slots)] * 4
        + [pltpu.SMEM((messages, 4, POINTS), jnp.float32), pltpu.SemaphoreType.DMA((2,))]
    )


def cost(microseconds):
    return pl.CostEstimate(flops=0, transcendentals=0, bytes_accessed=int(microseconds * 3.0e6))


def self_pairs(target, table):
    return pl.pallas_call(
        self_kernel,
        out_shape=[f32(*FORCE_SHAPE), f32(*COUNT_SHAPE)],
        in_specs=[VMEM, SMEM],
        out_specs=[VMEM] * 2,
        scratch_shapes=[pltpu.VMEM((CELLS * POINTS + STEP_ROWS, 8), jnp.float32)]
        + [list_space(CELLS)] * 2,
        compiler_params=PARAMS,
        cost_estimate=cost(6),
        name="self",
    )(target, table)


def near_pairs(target, table, from_even, from_odd, force, counts):
    return pl.pallas_call(
        near_kernel,
        out_shape=[f32(*FORCE_SHAPE), f32(*COUNT_SHAPE)],
        in_specs=[VMEM, SMEM] + [VMEM] * 4,
        out_specs=[VMEM] * 2,
        scratch_shapes=ghost_space(2),
        input_output_aliases={4: 0, 5: 1},
        compiler_params=PARAMS,
        cost_estimate=cost(4),
        name="near",
    )(target, table, from_even, from_odd, force, counts)


def far_pairs(devices, target, table, from_even, from_odd, force, counts):
    return pl.pallas_call(
        far_kernel,
        out_shape=[f32(*FORCE_SHAPE), f32(*COUNT_SHAPE), f32(*GRAD_SHAPE), f32(devices, 2, POINTS)],
        in_specs=[VMEM, SMEM] + [VMEM] * 4,
        out_specs=[VMEM] * 4,
        scratch_shapes=ghost_space(6),
        input_output_aliases={4: 0, 5: 1},
        compiler_params=PARAMS,
        cost_estimate=cost(12),
        name="far",
    )(target, table, from_even, from_odd, force, counts)[2:]


def body(positions, cell_points, target_log, export_count, export_cell, import_pair, import_shift):
    devices = export_count.shape[1]
    inputs = (
        positions, cell_points, target_log, export_count,
        jnp.transpose(export_cell, (2, 0, 1)),
        jnp.transpose(import_pair, (2, 0, 1)),
        jnp.transpose(import_shift, (0, 3, 1, 2)),
    )
    target, logs, table, *messages = pl.pallas_call(
        first_kernel,
        out_shape=[f32(*CELL_SHAPE), f32(BINS, POINTS), jax.ShapeDtypeStruct((TABLE,), jnp.int32)] + MESSAGES,
        in_specs=[pl.BlockSpec(memory_space=pltpu.HBM)] * 7,
        out_specs=[VMEM, VMEM, SMEM] + [VMEM] * 4,
        scratch_shapes=[
            pltpu.VMEM(positions.shape, jnp.float32),
            pltpu.SMEM(cell_points.shape, jnp.int32),
            pltpu.SMEM(target_log.shape, jnp.float32),
            pltpu.SMEM(export_count.shape, jnp.int32),
            pltpu.SMEM((SLOTS, 1, devices), jnp.int32),
            pltpu.SMEM((SLOTS, 1, devices), jnp.int32),
            pltpu.SMEM((3, SLOTS, 1, devices), jnp.int32),
            pltpu.VMEM(CELL_SHAPE, jnp.float32),
            pltpu.SemaphoreType.DMA((7,)),
        ],
        compiler_params=PARAMS,
        name="first",
    )(*(pltpu.with_memory_space_constraint(value, pltpu.HBM) for value in inputs))
    for iteration in range(STEPS):
        sky_even, sky_odd, depth_even, depth_odd = messages
        sky_even, sky_odd = swap(sky_even, "sky", 1), swap(sky_odd, "sky", 2)
        sky_even, sky_odd, force, counts = lax.optimization_barrier(
            (sky_even, sky_odd, *self_pairs(target, table))
        )
        near = near_pairs(target, table, sky_even, sky_odd, force, counts)
        depth_even = swap(jnp.stack([depth_even, sky_even[1], sky_odd[1]]), "depth", 1)
        depth_odd = swap(jnp.stack([depth_odd, sky_even[2], sky_odd[2]]), "depth", 2)
        grad, payload = far_pairs(devices, target, table, depth_even, depth_odd, *near)
        sums = lax.all_to_all(payload, AXES, 0, 0)
        if iteration == STEPS - 1:
            return pl.pallas_call(
                last_kernel,
                out_shape=f32(*positions.shape),
                in_specs=[VMEM] * 4,
                out_specs=VMEM,
                compiler_params=PARAMS,
                name="last",
            )(sums, grad, travel, logs)
        travel, target, *messages = pl.pallas_call(
            update_kernel,
            out_shape=[f32(*CELL_SHAPE), f32(*CELL_SHAPE)] + MESSAGES,
            in_specs=[VMEM] * 4 + [SMEM],
            out_specs=[VMEM] * 6,
            scratch_shapes=[pltpu.VMEM(CELL_SHAPE, jnp.float32)],
            compiler_params=PARAMS,
            name="update",
        )(sums, grad, target, logs, table)


def solution(mesh):
    in_specs = (
        P(None, ("sky", "depth"), None),
        P(("sky", "depth")),
        P(),
        P(("sky", "depth"), None),
        P(("sky", "depth"), None, None),
        P(("sky", "depth"), None, None),
        P(None, ("sky", "depth"), None, None),
    )
    out_specs = P(None, ("sky", "depth"), None)
    return jax.shard_map(body, mesh=mesh, in_specs=in_specs, out_specs=out_specs, check_vma=False)
```
